512 devices in a mesh: lat: 64 (over z, y), wid: 2 (over core), tok: 4 (over x).
Axes of the slice: x: 4, y: 4, z: 16, core: 2. Of those that a mesh axis runs over, the one named last changes fastest.
Arguments:
- resid: bfloat16 [512, 4096], P('tok', 'wid'), may hold values from -6 to 6
- dictionary: bfloat16 [32768, 4096], P('lat', 'wid'), may hold values from -0.1875 to 0.1875
- enc_bias: float32 [32768], P('lat'), may hold values from -3 to 3
- dec_bias: float32 [4096], P('wid'), may hold values from -3 to 3
- active_blocks: int32 [512, 8], P('tok'), may hold values from 0 to 255, all different within a row
- level_bounds: int32 [4], replicated, may hold values from 1 to 256, as said below
Outputs:
- level_losses: float32 [4], replicated
- dict_grad: bfloat16 [4096, 32768], P(('wid', 'tok'), 'lat')
The draws below stay inside these ranges and needn't reach their ends.
Inputs may be any that keep to these rules, and one draw needn't show every extreme that they name: `active_blocks`: each row names 8 different blocks. `level_bounds`: strictly increasing; the last equals 256.
All inputs are finite; a program needn't handle non-finite values.
Results may differ from the reference program's by a relative error of at most 0.006.
Values sent between devices are 32-bit elements; how exact they have to be, the bound alone decides.
A program may use at most 192 MiB of HBM per device.

```python
import jax
import jax.numpy as jnp
from jax import lax

D = 4096
KB = 8
LEVELS = 4
TOKENS = 512
LATENTS = 32768
BLOCKS = 256


def draw_level_bounds(key, part):
    shuffled = jax.random.permutation(key, BLOCKS - 1) + 1
    picked = jnp.sort(shuffled[:LEVELS - 1]).astype(jnp.int32)
    return jnp.concatenate([picked, jnp.array([BLOCKS], jnp.int32)])


def block_levels(own_key, dims, cuts, low, largest):
    gain = 1.0
    for axis_at, shards_of in cuts:
        draws = jax.random.uniform(jax.random.fold_in(jax.random.fold_in(own_key, 6), axis_at), (shards_of,), jnp.float32, low / len(cuts), largest / len(cuts))
        gain = gain * jnp.repeat(jnp.exp(draws), dims[axis_at] // shards_of).reshape((-1,) + (1,) * (len(dims) - 1 - axis_at))
    return gain


def different_ones(key, rows, amount, top, lift):
    order = jax.random.permutation(jax.random.fold_in(key, 1), amount)
    boost = order
    for power in range(3):
        boost = boost * boost // amount
    boost = boost * lift // amount
    chance = jax.random.randint(jax.random.fold_in(key, 2), (rows, amount), 0, 4096) + boost
    sure = jax.random.permutation(jax.random.fold_in(key, 3), rows)[jnp.arange(amount) % rows]
    chance = jnp.where(jnp.arange(rows)[:, None] == sure[None, :], 1 << 14, chance)
    score = chance * amount + jnp.arange(amount)
    return lax.top_k(score.astype(jnp.int32), top)[1].astype(jnp.int32)


def noise(stream_key, dims, scale, most, shards=(), kind=jnp.bfloat16):
    values = jax.random.normal(stream_key, dims, jnp.float32) * scale
    if len(shards) > 0:
        values = block_levels(stream_key, dims, shards, -0.22, 0.18) * values
    return jnp.clip(values, min=-most, max=most).astype(kind)


def setup_inputs(seed: int = 0) -> dict:
    key_of = jax.random.split(jax.random.key(seed), 7)
    resid = noise(key_of[0], (TOKENS, D), 1.0, 6.0, ((0, 4), (1, 2)))
    dictionary = noise(key_of[1], (LATENTS, D), (KB * 128) ** -0.5, 0.1875, ((0, 64), (1, 2)))
    enc_bias = noise(key_of[2], (LATENTS,), 0.5, 3.0, ((0, 64),), jnp.float32)
    dec_bias = noise(key_of[3], (D,), 0.5, 3.0, ((0, 2),), jnp.float32)
    active_blocks = different_ones(key_of[4], TOKENS, BLOCKS, KB, 512)
    level_bounds = draw_level_bounds(jax.random.fold_in(key_of[6], 71), 0)
    return {"resid": resid, "dictionary": dictionary, "enc_bias": enc_bias, "dec_bias": dec_bias, "active_blocks": active_blocks, "level_bounds": level_bounds}


def gelu_tanh(value):
    return jax.nn.gelu(value, approximate=True)

def reference(resid, dictionary, enc_bias, dec_bias, active_blocks, level_bounds):
    token_count, width = resid.shape
    block_count = dictionary.shape[0] // 128
    resid_full = resid.astype(jnp.float32)
    dict_blocks = dictionary.reshape(block_count, 128, width)
    bias_blocks = enc_bias.reshape(block_count, 128)
    block_ids = jnp.arange(block_count, dtype=jnp.int32)

    def encode(w_block, b_block, block_id):
        pre = jnp.dot(resid, w_block.T, preferred_element_type=jnp.float32) + b_block[None, :]
        hit = jnp.any(active_blocks == block_id, axis=1).astype(jnp.float32)
        return (pre, hit)

    def forward(carry, item):
        running, levels = carry
        w_block, b_block, block_id = item
        pre, hit = encode(w_block, b_block, block_id)
        act = (gelu_tanh(pre) * hit[:, None]).astype(jnp.bfloat16)
        running = running + jnp.dot(act, w_block, preferred_element_type=jnp.float32)
        finished = level_bounds == block_id + 1
        levels = jnp.where(finished[:, None, None], running[None], levels)
        return ((running, levels), None)
    start = (jnp.zeros((token_count, width), jnp.float32), jnp.zeros((LEVELS, token_count, width), jnp.float32))
    (running, levels), _ = lax.scan(forward, start, (dict_blocks, bias_blocks, block_ids))
    errors = dec_bias[None, None, :] + levels - resid_full[None]
    level_losses = lax.optimization_barrier(jnp.sum(errors * errors, axis=(1, 2))) / (token_count * width)
    cum_err = jnp.cumsum(errors[::-1], axis=0)[::-1].astype(jnp.bfloat16)

    def backward(carry, item):
        w_block, b_block, block_id = item
        pre, hit = encode(w_block, b_block, block_id)
        act = (gelu_tanh(pre) * hit[:, None]).astype(jnp.bfloat16)
        level_of = jnp.sum((level_bounds <= block_id).astype(jnp.int32)).astype(jnp.int32)
        err_block = lax.dynamic_index_in_dim(cum_err, level_of, 0, keepdims=False)
        g_act = jnp.dot(err_block, w_block.T, preferred_element_type=jnp.float32)
        _, pull = jax.vjp(gelu_tanh, pre)
        g_pre = pull(g_act * hit[:, None])[0].astype(jnp.bfloat16)
        grad = jnp.dot(err_block.T, act, preferred_element_type=jnp.float32)
        grad = grad + jnp.dot(resid.T, g_pre, preferred_element_type=jnp.float32)
        return (carry, grad.astype(jnp.bfloat16))
    _, grads = lax.scan(backward, 0, (dict_blocks, bias_blocks, block_ids))
    dict_grad = jnp.transpose(grads, (1, 0, 2)).reshape(width, block_count * 128)
    return (level_losses, dict_grad)
```

```python
import functools

import jax
import jax.numpy as jnp
from jax import lax
from jax.experimental import pallas as pl
from jax.experimental.pallas import tpu as pltpu
from jax.sharding import PartitionSpec as P

LEVELS = 4
MESH_ID = pl.DeviceIdType.MESH


def gelu_tanh(value):
    return jax.nn.gelu(value, approximate=True)


def device_on(axis_names, moved):
    return tuple(moved[n] if n in moved else lax.axis_index(n) for n in axis_names)


def pair_sum_kernel(axis_names, x_ref, out_ref, held, send_sem, recv_sem):
    me = lax.axis_index("wid")
    other = device_on(axis_names, {"wid": 1 - me})
    barrier = pltpu.get_barrier_semaphore()
    pl.semaphore_signal(barrier, 1, device_id=other, device_id_type=MESH_ID)
    pl.semaphore_wait(barrier, 1)
    copy = pltpu.make_async_remote_copy(
        src_ref=x_ref, dst_ref=held, send_sem=send_sem, recv_sem=recv_sem,
        device_id=other, device_id_type=MESH_ID,
    )
    copy.start()
    copy.wait()
    out_ref[...] = x_ref[...] + held[...]


def pair_sum(x, axis_names, cid):
    return pl.pallas_call(
        functools.partial(pair_sum_kernel, axis_names),
        out_shape=jax.ShapeDtypeStruct(x.shape, x.dtype),
        in_specs=[pl.BlockSpec(memory_space=pltpu.VMEM)],
        out_specs=pl.BlockSpec(memory_space=pltpu.VMEM),
        scratch_shapes=[
            pltpu.VMEM(x.shape, x.dtype),
            pltpu.SemaphoreType.DMA(()),
            pltpu.SemaphoreType.DMA(()),
        ],
        compiler_params=pltpu.CompilerParams(collective_id=cid, has_side_effects=True),
    )(x)


def lat_sum_kernel(axis_names, ny, nz, x_ref, out_ref, recv1, ybuf, recv2, zbuf, yfull,
                   s1, r1, s2, r2, s3, r3, s4, r4):
    lat = lax.axis_index("lat")
    my_y = lat % ny
    my_z = lat // ny
    rows = x_ref.shape[1]
    cz = rows // nz

    def y_dev(c):
        return device_on(axis_names, {"lat": my_z * ny + c})

    def z_dev(c):
        return device_on(axis_names, {"lat": c * ny + my_y})

    def zrows(c):
        return pl.ds(pl.multiple_of(c * cz, cz), cz)

    barrier = pltpu.get_barrier_semaphore()
    for d in range(1, ny):
        pl.semaphore_signal(barrier, 1, device_id=y_dev((my_y + d) % ny), device_id_type=MESH_ID)
    for d in range(1, nz):
        pl.semaphore_signal(barrier, 1, device_id=z_dev((my_z + d) % nz), device_id_type=MESH_ID)
    pl.semaphore_wait(barrier, (ny - 1) + (nz - 1))

    sends = []
    for d in range(1, ny):
        c = (my_y + d) % ny
        cp = pltpu.make_async_remote_copy(
            src_ref=x_ref.at[c], dst_ref=recv1.at[my_y], send_sem=s1.at[c], recv_sem=r1.at[my_y],
            device_id=y_dev(c), device_id_type=MESH_ID,
        )
        cp.start()
        sends.append(cp)
    recv1[my_y] = x_ref[my_y]
    for d in range(1, ny):
        src = (my_y + ny - d) % ny
        pltpu.make_async_remote_copy(
            src_ref=x_ref.at[src], dst_ref=recv1.at[src], send_sem=s1.at[src], recv_sem=r1.at[src],
            device_id=y_dev(src), device_id_type=MESH_ID,
        ).wait_recv()
    total = recv1[0]
    for s in range(1, ny):
        total = total + recv1[s]
    ybuf[...] = total
    for cp in sends:
        cp.wait_send()

    sends = []
    for d in range(1, nz):
        c = (my_z + d) % nz
        cp = pltpu.make_async_remote_copy(
            src_ref=ybuf.at[zrows(c)], dst_ref=recv2.at[my_z], send_sem=s2.at[c], recv_sem=r2.at[my_z],
            device_id=z_dev(c), device_id_type=MESH_ID,
        )
        cp.start()
        sends.append(cp)
    recv2[my_z] = ybuf[zrows(my_z)]
    for d in range(1, nz):
        src = (my_z + nz - d) % nz
        pltpu.make_async_remote_copy(
            src_ref=ybuf.at[zrows(src)], dst_ref=recv2.at[src], send_sem=s2.at[src], recv_sem=r2.at[src],
            device_id=z_dev(src), device_id_type=MESH_ID,
        ).wait_recv()
    total = recv2[0]
    for s in range(1, nz):
        total = total + recv2[s]
    zbuf[...] = total
    for cp in sends:
        cp.wait_send()

    sends = []
    for d in range(1, nz):
        c = (my_z + d) % nz
        cp = pltpu.make_async_remote_copy(
            src_ref=zbuf, dst_ref=yfull.at[zrows(my_z)], send_sem=s3.at[c], recv_sem=r3.at[my_z],
            device_id=z_dev(c), device_id_type=MESH_ID,
        )
        cp.start()
        sends.append(cp)
    yfull[zrows(my_z)] = zbuf[...]
    for d in range(1, nz):
        src = (my_z + nz - d) % nz
        pltpu.make_async_remote_copy(
            src_ref=zbuf, dst_ref=yfull.at[zrows(src)], send_sem=s3.at[src], recv_sem=r3.at[src],
            device_id=z_dev(src), device_id_type=MESH_ID,
        ).wait_recv()
    for cp in sends:
        cp.wait_send()

    sends = []
    for d in range(1, ny):
        c = (my_y + d) % ny
        cp = pltpu.make_async_remote_copy(
            src_ref=yfull, dst_ref=out_ref.at[my_y], send_sem=s4.at[c], recv_sem=r4.at[my_y],
            device_id=y_dev(c), device_id_type=MESH_ID,
        )
        cp.start()
        sends.append(cp)
    out_ref[my_y] = yfull[...]
    for d in range(1, ny):
        src = (my_y + ny - d) % ny
        pltpu.make_async_remote_copy(
            src_ref=yfull, dst_ref=out_ref.at[src], send_sem=s4.at[src], recv_sem=r4.at[src],
            device_id=y_dev(src), device_id_type=MESH_ID,
        ).wait_recv()
    for cp in sends:
        cp.wait_send()


def lat_sum(x, axis_names, n_lat, cid):
    ny = 4 if n_lat % 4 == 0 else 1
    nz = n_lat // ny
    chunks, rows, width = x.shape
    assert chunks == ny and rows % (8 * nz) == 0
    cz = rows // nz
    f32 = jnp.float32
    return pl.pallas_call(
        functools.partial(lat_sum_kernel, axis_names, ny, nz),
        out_shape=jax.ShapeDtypeStruct(x.shape, x.dtype),
        in_specs=[pl.BlockSpec(memory_space=pltpu.VMEM)],
        out_specs=pl.BlockSpec(memory_space=pltpu.VMEM),
        scratch_shapes=[
            pltpu.VMEM((ny, rows, width), f32),
            pltpu.VMEM((rows, width), f32),
            pltpu.VMEM((nz, cz, width), f32),
            pltpu.VMEM((cz, width), f32),
            pltpu.VMEM((rows, width), f32),
            pltpu.SemaphoreType.DMA((ny,)),
            pltpu.SemaphoreType.DMA((ny,)),
            pltpu.SemaphoreType.DMA((nz,)),
            pltpu.SemaphoreType.DMA((nz,)),
            pltpu.SemaphoreType.DMA((nz,)),
            pltpu.SemaphoreType.DMA((nz,)),
            pltpu.SemaphoreType.DMA((ny,)),
            pltpu.SemaphoreType.DMA((ny,)),
        ],
        compiler_params=pltpu.CompilerParams(
            collective_id=cid, has_side_effects=True, vmem_limit_bytes=48 * 1024 * 1024
        ),
    )(x)


def body(axis_names, n_lat, resid, dictionary, enc_bias, dec_bias, active_blocks, level_bounds):
    row_count, half_width = resid.shape
    lat_count = dictionary.shape[0]
    blocks_here = lat_count // 128
    lat_position = lax.axis_index("lat")
    first_block = lat_position * blocks_here
    local_ids = first_block + jnp.arange(blocks_here, dtype=jnp.int32)
    resid_full = resid.astype(jnp.float32)
    dict_blocks = dictionary.reshape(blocks_here, 128, half_width)

    partial_pre = lax.dot_general(
        resid, dictionary, (((1,), (1,)), ((), ())), preferred_element_type=jnp.float32
    )
    pre = pair_sum(partial_pre, axis_names, 1) + enc_bias[None, :]
    hits = jnp.any(active_blocks[:, :, None] == local_ids[None, None, :], axis=1).astype(
        jnp.float32
    )
    act = (gelu_tanh(pre).reshape(row_count, blocks_here, 128) * hits[:, :, None]).astype(
        jnp.bfloat16
    )
    act_flat = act.reshape(row_count, lat_count)

    latent_block = first_block + jnp.arange(lat_count, dtype=jnp.int32) // 128
    keep = latent_block[None, :] < level_bounds[:, None]
    act_stack = jnp.where(keep[:, None, :], act_flat[None], jnp.zeros((), jnp.bfloat16))
    contrib = jnp.dot(
        act_stack.reshape(LEVELS * row_count, lat_count),
        dictionary,
        preferred_element_type=jnp.float32,
    ).reshape(LEVELS, row_count, half_width)
    levels = lat_sum(contrib, axis_names, n_lat, 0)

    errors = dec_bias[None, None, :] + levels - resid_full[None]
    squares = jnp.sum(errors * errors, axis=(1, 2))
    total_sq = lax.psum(squares, ("wid", "tok"))
    level_losses = total_sq / (row_count * lax.axis_size("tok") * half_width * lax.axis_size("wid"))
    cum_err = jnp.cumsum(errors[::-1], axis=0)[::-1].astype(jnp.bfloat16)

    level_of = jnp.sum((level_bounds[None, :] <= local_ids[:, None]).astype(jnp.int32), axis=1)
    err_half = jnp.take(cum_err, level_of, axis=0)
    partial_adjoint = jnp.einsum(
        "ktd,kcd->tkc", err_half, dict_blocks, preferred_element_type=jnp.float32
    )
    g_act = pair_sum(partial_adjoint.reshape(row_count, lat_count), axis_names, 2)
    mask_full = jnp.broadcast_to(hits[:, :, None], (row_count, blocks_here, 128)).reshape(
        row_count, lat_count
    )
    _, pull = jax.vjp(gelu_tanh, pre)
    g_pre = pull(g_act * mask_full)[0].astype(jnp.bfloat16)
    decode_term = jnp.einsum("ktd,tkc->dkc", err_half, act, preferred_element_type=jnp.float32)
    encode_term = lax.dot_general(
        resid, g_pre, (((0,), (0,)), ((), ())), preferred_element_type=jnp.float32
    )
    grad_share = lax.psum_scatter(
        decode_term.reshape(half_width, lat_count) + encode_term,
        "tok",
        scatter_dimension=0,
        tiled=True,
    )
    return (level_losses, grad_share.astype(jnp.bfloat16))


def solution(mesh):
    axis_names = tuple(mesh.axis_names)
    n_lat = mesh.shape["lat"]
    return jax.shard_map(
        functools.partial(body, axis_names, n_lat),
        mesh=mesh,
        in_specs=(P("tok", "wid"), P("lat", "wid"), P("lat"), P("wid"), P("tok", None), P()),
        out_specs=(P(), P(("wid", "tok"), "lat")),
        check_vma=False,
    )
```

```python
import functools

import jax
import jax.numpy as jnp
from jax import lax
from jax.experimental import pallas as pl
from jax.experimental.pallas import tpu as pltpu
from jax.sharding import PartitionSpec as P

LEVELS = 4
MESH_ID = pl.DeviceIdType.MESH


def gelu_tanh(value):
    return jax.nn.gelu(value, approximate=True)


def device_on(axis_names, moved):
    return tuple(moved[n] if n in moved else lax.axis_index(n) for n in axis_names)


def remote(src, dst, send_sem, recv_sem, device):
    return pltpu.make_async_remote_copy(
        src_ref=src, dst_ref=dst, send_sem=send_sem, recv_sem=recv_sem,
        device_id=device, device_id_type=MESH_ID,
    )


def gather_phase(n, pos, dev_of, src_of, slot_of, send_sems, recv_sems):
    sends = []
    for d in range(1, n):
        c = (pos + d) % n
        cp = remote(src_of(c), slot_of(pos), send_sems.at[c], recv_sems.at[pos], dev_of(c))
        cp.start()
        sends.append(cp)
    slot_of(pos)[...] = src_of(pos)[...]
    for d in range(1, n):
        s = (pos + n - d) % n
        remote(src_of(s), slot_of(s), send_sems.at[s], recv_sems.at[s], dev_of(s)).wait_recv()
    return sends


def axis_sum_kernel(axis_names, axis, n, x_ref, out_ref, slots, send_sem, recv_sem):
    me = lax.axis_index(axis)

    def dev_of(c):
        return device_on(axis_names, {axis: c})

    barrier = pltpu.get_barrier_semaphore()
    for d in range(1, n):
        pl.semaphore_signal(barrier, 1, device_id=dev_of((me + d) % n), device_id_type=MESH_ID)
    pl.semaphore_wait(barrier, n - 1)
    sends = gather_phase(n, me, dev_of, lambda c: x_ref, lambda c: slots.at[c], send_sem, recv_sem)
    total = slots[0]
    for s in range(1, n):
        total = total + slots[s]
    out_ref[...] = total
    for cp in sends:
        cp.wait_send()


def axis_sum(x, axis_names, axis, n, cid):
    return pl.pallas_call(
        functools.partial(axis_sum_kernel, axis_names, axis, n),
        out_shape=jax.ShapeDtypeStruct(x.shape, x.dtype),
        in_specs=[pl.BlockSpec(memory_space=pltpu.VMEM)],
        out_specs=pl.BlockSpec(memory_space=pltpu.VMEM),
        scratch_shapes=[
            pltpu.VMEM((n,) + x.shape, x.dtype),
            pltpu.SemaphoreType.DMA((n,)),
            pltpu.SemaphoreType.DMA((n,)),
        ],
        compiler_params=pltpu.CompilerParams(collective_id=cid, has_side_effects=True),
    )(x)


def lat_sum_kernel(axis_names, ny, nlo, nhi, x_ref, out_ref, recv1, recv2, recv3, part3, part2, part1,
                   ag2, ag1, sems):
    lat = lax.axis_index("lat")
    my_y = lat % ny
    my_z = lat // ny
    my_lo = my_z % nlo
    my_hi = my_z // nlo
    rows = x_ref.shape[1]
    c2 = rows // nlo
    c3 = c2 // nhi

    def y_dev(c):
        return device_on(axis_names, {"lat": my_z * ny + c})

    def lo_dev(c):
        return device_on(axis_names, {"lat": (my_hi * nlo + c) * ny + my_y})

    def hi_dev(c):
        return device_on(axis_names, {"lat": (c * nlo + my_lo) * ny + my_y})

    def rows_of(c, size):
        return pl.ds(pl.multiple_of(c * size, size), size)

    barrier = pltpu.get_barrier_semaphore()
    for n, pos, dev_of in ((ny, my_y, y_dev), (nlo, my_lo, lo_dev), (nhi, my_hi, hi_dev)):
        for d in range(1, n):
            pl.semaphore_signal(barrier, 1, device_id=dev_of((pos + d) % n), device_id_type=MESH_ID)
    pl.semaphore_wait(barrier, (ny - 1) + (nlo - 1) + (nhi - 1))

    def summed(slots, n):
        total = slots[0]
        for s in range(1, n):
            total = total + slots[s]
        return total

    sends = gather_phase(ny, my_y, y_dev, lambda c: x_ref.at[c], lambda c: recv1.at[c],
                         sems.at[0, 0], sems.at[0, 1])
    part1[...] = summed(recv1, ny)
    for cp in sends:
        cp.wait_send()
    sends = gather_phase(nlo, my_lo, lo_dev, lambda c: part1.at[rows_of(c, c2)], lambda c: recv2.at[c],
                         sems.at[1, 0], sems.at[1, 1])
    part2[...] = summed(recv2, nlo)
    for cp in sends:
        cp.wait_send()
    sends = gather_phase(nhi, my_hi, hi_dev, lambda c: part2.at[rows_of(c, c3)], lambda c: recv3.at[c],
                         sems.at[2, 0], sems.at[2, 1])
    part3[...] = summed(recv3, nhi)
    for cp in sends:
        cp.wait_send()
    sends = gather_phase(nhi, my_hi, hi_dev, lambda c: part3, lambda c: ag2.at[rows_of(c, c3)],
                         sems.at[3, 0], sems.at[3, 1])
    for cp in sends:
        cp.wait_send()
    sends = gather_phase(nlo, my_lo, lo_dev, lambda c: ag2, lambda c: ag1.at[rows_of(c, c2)],
                         sems.at[4, 0], sems.at[4, 1])
    for cp in sends:
        cp.wait_send()
    sends = gather_phase(ny, my_y, y_dev, lambda c: ag1, lambda c: out_ref.at[c],
                         sems.at[5, 0], sems.at[5, 1])
    for cp in sends:
        cp.wait_send()


def lat_sum(x, axis_names, n_lat, cid):
    ny = 4 if n_lat % 4 == 0 else 1
    nz = n_lat // ny
    nlo = 4 if nz % 4 == 0 else nz
    nhi = nz // nlo
    chunks, rows, width = x.shape
    assert chunks == ny and rows % (8 * nz) == 0
    c2 = rows // nlo
    c3 = c2 // nhi
    f32 = jnp.float32
    most = max(ny, nlo, nhi)
    return pl.pallas_call(
        functools.partial(lat_sum_kernel, axis_names, ny, nlo, nhi),
        out_shape=jax.ShapeDtypeStruct(x.shape, x.dtype),
        in_specs=[pl.BlockSpec(memory_space=pltpu.VMEM)],
        out_specs=pl.BlockSpec(memory_space=pltpu.VMEM),
        scratch_shapes=[
            pltpu.VMEM((ny, rows, width), f32),
            pltpu.VMEM((nlo, c2, width), f32),
            pltpu.VMEM((nhi, c3, width), f32),
            pltpu.VMEM((c3, width), f32),
            pltpu.VMEM((c2, width), f32),
            pltpu.VMEM((rows, width), f32),
            pltpu.VMEM((c2, width), f32),
            pltpu.VMEM((rows, width), f32),
            pltpu.SemaphoreType.DMA((6, 2, most)),
        ],
        compiler_params=pltpu.CompilerParams(
            collective_id=cid, has_side_effects=True, vmem_limit_bytes=48 * 1024 * 1024
        ),
    )(x)


def body(axis_names, n_lat, resid, dictionary, enc_bias, dec_bias, active_blocks, level_bounds):
    row_count, half_width = resid.shape
    lat_count = dictionary.shape[0]
    blocks_here = lat_count // 128
    lat_position = lax.axis_index("lat")
    first_block = lat_position * blocks_here
    local_ids = first_block + jnp.arange(blocks_here, dtype=jnp.int32)
    resid_full = resid.astype(jnp.float32)
    dict_blocks = dictionary.reshape(blocks_here, 128, half_width)

    partial_pre = lax.dot_general(
        resid, dictionary, (((1,), (1,)), ((), ())), preferred_element_type=jnp.float32
    )
    pre = axis_sum(partial_pre, axis_names, "wid", 2, 1) + enc_bias[None, :]
    hits = jnp.any(active_blocks[:, :, None] == local_ids[None, None, :], axis=1).astype(
        jnp.float32
    )
    act = (gelu_tanh(pre).reshape(row_count, blocks_here, 128) * hits[:, :, None]).astype(
        jnp.bfloat16
    )
    act_flat = act.reshape(row_count, lat_count)

    latent_block = first_block + jnp.arange(lat_count, dtype=jnp.int32) // 128
    keep = latent_block[None, :] < level_bounds[:, None]
    act_stack = jnp.where(keep[:, None, :], act_flat[None], jnp.zeros((), jnp.bfloat16))
    contrib = jnp.dot(
        act_stack.reshape(LEVELS * row_count, lat_count),
        dictionary,
        preferred_element_type=jnp.float32,
    ).reshape(LEVELS, row_count, half_width)
    levels = lat_sum(contrib, axis_names, n_lat, 0)

    errors = dec_bias[None, None, :] + levels - resid_full[None]
    squares = jnp.sum(errors * errors, axis=(1, 2))
    running = errors[LEVELS - 1]
    cum_list = [running]
    for level in range(LEVELS - 2, -1, -1):
        running = running + errors[level]
        cum_list.append(running)
    cum_err = jnp.stack(cum_list[::-1]).astype(jnp.bfloat16)

    level_of = jnp.sum((level_bounds[None, :] <= local_ids[:, None]).astype(jnp.int32), axis=1)
    err_half = jnp.take(cum_err, level_of, axis=0)
    partial_adjoint = jnp.einsum(
        "ktd,kcd->tkc", err_half, dict_blocks, preferred_element_type=jnp.float32
    )
    loss_rows = jnp.zeros((8, lat_count), jnp.float32).at[0, :LEVELS].set(squares)
    adjoint_rows = jnp.concatenate([partial_adjoint.reshape(row_count, lat_count), loss_rows], axis=0)
    summed_rows = axis_sum(adjoint_rows, axis_names, "wid", 2, 2)
    g_act = summed_rows[:row_count]
    loss_tile = jnp.zeros((8, 128), jnp.float32).at[0, :LEVELS].set(summed_rows[row_count, :LEVELS])
    total_sq = axis_sum(loss_tile, axis_names, "tok", lax.axis_size("tok"), 3)[0, :LEVELS]
    level_losses = total_sq / (row_count * lax.axis_size("tok") * half_width * lax.axis_size("wid"))
    mask_full = jnp.broadcast_to(hits[:, :, None], (row_count, blocks_here, 128)).reshape(
        row_count, lat_count
    )
    _, pull = jax.vjp(gelu_tanh, pre)
    g_pre = pull(g_act * mask_full)[0].astype(jnp.bfloat16)
    decode_term = jnp.einsum("ktd,tkc->dkc", err_half, act, preferred_element_type=jnp.float32)
    encode_term = lax.dot_general(
        resid, g_pre, (((0,), (0,)), ((), ())), preferred_element_type=jnp.float32
    )
    grad_share = lax.psum_scatter(
        decode_term.reshape(half_width, lat_count) + encode_term,
        "tok",
        scatter_dimension=0,
        tiled=True,
    )
    return (level_losses, grad_share.astype(jnp.bfloat16))


def solution(mesh):
    axis_names = tuple(mesh.axis_names)
    n_lat = mesh.shape["lat"]
    return jax.shard_map(
        functools.partial(body, axis_names, n_lat),
        mesh=mesh,
        in_specs=(P("tok", "wid"), P("lat", "wid"), P("lat"), P("wid"), P("tok", None), P()),
        out_specs=(P(), P(("wid", "tok"), "lat")),
        check_vma=False,
    )
```

```python
import functools

import jax
import jax.numpy as jnp
from jax import lax
from jax.experimental import pallas as pl
from jax.experimental.pallas import tpu as pltpu
from jax.sharding import PartitionSpec as P

LEVELS = 4
MESH_ID = pl.DeviceIdType.MESH


def gelu_tanh(value):
    return jax.nn.gelu(value, approximate=True)


def device_on(axis_names, moved):
    return tuple(moved[n] if n in moved else lax.axis_index(n) for n in axis_names)


def remote(src, dst, send_sem, recv_sem, device):
    return pltpu.make_async_remote_copy(
        src_ref=src, dst_ref=dst, send_sem=send_sem, recv_sem=recv_sem,
        device_id=device, device_id_type=MESH_ID,
    )


def gather_phase(n, pos, dev_of, src_of, slot_of, send_sems, recv_sems):
    sends = []
    for d in range(1, n):
        c = (pos + d) % n
        cp = remote(src_of(c), slot_of(pos), send_sems.at[c], recv_sems.at[pos], dev_of(c))
        cp.start()
        sends.append(cp)
    slot_of(pos)[...] = src_of(pos)[...]
    for d in range(1, n):
        s = (pos + n - d) % n
        remote(src_of(s), slot_of(s), send_sems.at[s], recv_sems.at[s], dev_of(s)).wait_recv()
    return sends


def ring_reduce_scatter(n, pos, dev_of, src, recv, acc, sems, put):
    half = src.shape[1] // 2
    dirs = (1, n - 1)
    sends = []
    for s in range(n - 1):
        for h, dr in enumerate(dirs):
            k = (pos + (s + 1) * (n - dr)) % n
            source = src.at[k, pl.ds(h * half, half)] if s == 0 else acc.at[h, s - 1]
            cp = remote(source, recv.at[h, s], sems.at[h, 0, s], sems.at[h, 1, s], dev_of((pos + dr) % n))
            cp.start()
            sends.append(cp)
        for h, dr in enumerate(dirs):
            k2 = (pos + (s + 2) * (n - dr)) % n
            own = src.at[k2, pl.ds(h * half, half)]
            remote(own, recv.at[h, s], sems.at[h, 0, s], sems.at[h, 1, s],
                   dev_of((pos + n - dr) % n)).wait_recv()
            new = recv[h, s] + own[...]
            if s < n - 2:
                acc[h, s] = new
            else:
                put(h, new)
    return sends


def ring_all_gather(n, pos, dev_of, mine, dst, sems):
    half = mine.shape[0] // 2
    dirs = (1, n - 1)
    dst[pos] = mine[...]
    sends = []
    for s in range(n - 1):
        for h, dr in enumerate(dirs):
            k = (pos + s * (n - dr)) % n
            rows = pl.ds(h * half, half)
            source = mine.at[rows] if s == 0 else dst.at[k, rows]
            cp = remote(source, dst.at[k, rows], sems.at[h, 0, s], sems.at[h, 1, s], dev_of((pos + dr) % n))
            cp.start()
            sends.append(cp)
        for h, dr in enumerate(dirs):
            k2 = (pos + (s + 1) * (n - dr)) % n
            rows = pl.ds(h * half, half)
            remote(mine.at[rows], dst.at[k2, rows], sems.at[h, 0, s], sems.at[h, 1, s],
                   dev_of((pos + n - dr) % n)).wait_recv()
    return sends


def ring_sum_kernel(axis_names, axis, n, x_ref, out_ref, recv, acc, sems):
    me = lax.axis_index(axis)

    def dev_of(c):
        return device_on(axis_names, {axis: c})

    barrier = pltpu.get_barrier_semaphore()
    for d in range(1, n):
        pl.semaphore_signal(barrier, 1, device_id=dev_of((me + d) % n), device_id_type=MESH_ID)
    pl.semaphore_wait(barrier, n - 1)
    half = x_ref.shape[1] // 2

    def put(h, value):
        out_ref[pl.ds(h * half, half)] = value.astype(out_ref.dtype)

    sends = ring_reduce_scatter(n, me, dev_of, x_ref, recv, acc, sems, put)
    for cp in sends:
        cp.wait_send()


def ring_sum_scatter(x, axis_names, axis, n, cid, out_dtype):
    _, rows, width = x.shape
    return pl.pallas_call(
        functools.partial(ring_sum_kernel, axis_names, axis, n),
        out_shape=jax.ShapeDtypeStruct((rows, width), out_dtype),
        in_specs=[pl.BlockSpec(memory_space=pltpu.VMEM)],
        out_specs=pl.BlockSpec(memory_space=pltpu.VMEM),
        scratch_shapes=[
            pltpu.VMEM((2, n - 1, rows // 2, width), x.dtype),
            pltpu.VMEM((2, max(n - 2, 1), rows // 2, width), x.dtype),
            pltpu.SemaphoreType.DMA((2, 2, n - 1)),
        ],
        compiler_params=pltpu.CompilerParams(
            collective_id=cid, has_side_effects=True, vmem_limit_bytes=48 * 1024 * 1024
        ),
    )(x)


def axis_sum_kernel(axis_names, axis, n, x_ref, out_ref, slots, send_sem, recv_sem):
    me = lax.axis_index(axis)

    def dev_of(c):
        return device_on(axis_names, {axis: c})

    barrier = pltpu.get_barrier_semaphore()
    for d in range(1, n):
        pl.semaphore_signal(barrier, 1, device_id=dev_of((me + d) % n), device_id_type=MESH_ID)
    pl.semaphore_wait(barrier, n - 1)
    sends = gather_phase(n, me, dev_of, lambda c: x_ref, lambda c: slots.at[c], send_sem, recv_sem)
    total = slots[0]
    for s in range(1, n):
        total = total + slots[s]
    out_ref[...] = total
    for cp in sends:
        cp.wait_send()


def axis_sum(x, axis_names, axis, n, cid):
    return pl.pallas_call(
        functools.partial(axis_sum_kernel, axis_names, axis, n),
        out_shape=jax.ShapeDtypeStruct(x.shape, x.dtype),
        in_specs=[pl.BlockSpec(memory_space=pltpu.VMEM)],
        out_specs=pl.BlockSpec(memory_space=pltpu.VMEM),
        scratch_shapes=[
            pltpu.VMEM((n,) + x.shape, x.dtype),
            pltpu.SemaphoreType.DMA((n,)),
            pltpu.SemaphoreType.DMA((n,)),
        ],
        compiler_params=pltpu.CompilerParams(collective_id=cid, has_side_effects=True),
    )(x)


def lat_sum_kernel(axis_names, ny, nlo, nhi, x_ref, out_ref, recv1, acc1, recv2, recv3, part3, part2,
                   part1, ag2, ag1, sems, ring_sems):
    lat = lax.axis_index("lat")
    my_y = lat % ny
    my_z = lat // ny
    my_lo = my_z % nlo
    my_hi = my_z // nlo
    rows = x_ref.shape[1]
    c2 = rows // nlo
    c3 = c2 // nhi

    def y_dev(c):
        return device_on(axis_names, {"lat": my_z * ny + c})

    def lo_dev(c):
        return device_on(axis_names, {"lat": (my_hi * nlo + c) * ny + my_y})

    def hi_dev(c):
        return device_on(axis_names, {"lat": (c * nlo + my_lo) * ny + my_y})

    def rows_of(c, size):
        return pl.ds(pl.multiple_of(c * size, size), size)

    barrier = pltpu.get_barrier_semaphore()
    for n, pos, dev_of in ((ny, my_y, y_dev), (nlo, my_lo, lo_dev), (nhi, my_hi, hi_dev)):
        for d in range(1, n):
            pl.semaphore_signal(barrier, 1, device_id=dev_of((pos + d) % n), device_id_type=MESH_ID)
    pl.semaphore_wait(barrier, (ny - 1) + (nlo - 1) + (nhi - 1))

    def summed(slots, n):
        total = slots[0]
        for s in range(1, n):
            total = total + slots[s]
        return total

    half = rows // 2

    def put(h, value):
        part1[pl.ds(h * half, half)] = value

    sends = ring_reduce_scatter(ny, my_y, y_dev, x_ref, recv1, acc1, ring_sems.at[0], put)
    for cp in sends:
        cp.wait_send()
    sends = gather_phase(nlo, my_lo, lo_dev, lambda c: part1.at[rows_of(c, c2)], lambda c: recv2.at[c],
                         sems.at[1, 0], sems.at[1, 1])
    part2[...] = summed(recv2, nlo)
    for cp in sends:
        cp.wait_send()
    sends = gather_phase(nhi, my_hi, hi_dev, lambda c: part2.at[rows_of(c, c3)], lambda c: recv3.at[c],
                         sems.at[2, 0], sems.at[2, 1])
    part3[...] = summed(recv3, nhi)
    for cp in sends:
        cp.wait_send()
    sends = gather_phase(nhi, my_hi, hi_dev, lambda c: part3, lambda c: ag2.at[rows_of(c, c3)],
                         sems.at[3, 0], sems.at[3, 1])
    for cp in sends:
        cp.wait_send()
    sends = gather_phase(nlo, my_lo, lo_dev, lambda c: ag2, lambda c: ag1.at[rows_of(c, c2)],
                         sems.at[4, 0], sems.at[4, 1])
    for cp in sends:
        cp.wait_send()
    sends = ring_all_gather(ny, my_y, y_dev, ag1, out_ref, ring_sems.at[1])
    for cp in sends:
        cp.wait_send()


def lat_sum(x, axis_names, n_lat, cid):
    ny = 4 if n_lat % 4 == 0 else 1
    nz = n_lat // ny
    nlo = 4 if nz % 4 == 0 else nz
    nhi = nz // nlo
    chunks, rows, width = x.shape
    assert chunks == ny and rows % (8 * nz) == 0
    c2 = rows // nlo
    c3 = c2 // nhi
    f32 = jnp.float32
    most = max(ny, nlo, nhi)
    return pl.pallas_call(
        functools.partial(lat_sum_kernel, axis_names, ny, nlo, nhi),
        out_shape=jax.ShapeDtypeStruct(x.shape, x.dtype),
        in_specs=[pl.BlockSpec(memory_space=pltpu.VMEM)],
        out_specs=pl.BlockSpec(memory_space=pltpu.VMEM),
        scratch_shapes=[
            pltpu.VMEM((2, ny - 1, rows // 2, width), f32),
            pltpu.VMEM((2, max(ny - 2, 1), rows // 2, width), f32),
            pltpu.VMEM((nlo, c2, width), f32),
            pltpu.VMEM((nhi, c3, width), f32),
            pltpu.VMEM((c3, width), f32),
            pltpu.VMEM((c2, width), f32),
            pltpu.VMEM((rows, width), f32),
            pltpu.VMEM((c2, width), f32),
            pltpu.VMEM((rows, width), f32),
            pltpu.SemaphoreType.DMA((6, 2, most)),
            pltpu.SemaphoreType.DMA((2, 2, 2, ny - 1)),
        ],
        compiler_params=pltpu.CompilerParams(
            collective_id=cid, has_side_effects=True, vmem_limit_bytes=48 * 1024 * 1024
        ),
    )(x)


def body(axis_names, n_lat, resid, dictionary, enc_bias, dec_bias, active_blocks, level_bounds):
    row_count, half_width = resid.shape
    lat_count = dictionary.shape[0]
    blocks_here = lat_count // 128
    lat_position = lax.axis_index("lat")
    first_block = lat_position * blocks_here
    local_ids = first_block + jnp.arange(blocks_here, dtype=jnp.int32)
    resid_full = resid.astype(jnp.float32)
    dict_blocks = dictionary.reshape(blocks_here, 128, half_width)

    partial_pre = lax.dot_general(
        resid, dictionary, (((1,), (1,)), ((), ())), preferred_element_type=jnp.float32
    )
    pre = axis_sum(partial_pre, axis_names, "wid", 2, 1) + enc_bias[None, :]
    hits = jnp.any(active_blocks[:, :, None] == local_ids[None, None, :], axis=1).astype(
        jnp.float32
    )
    act = (gelu_tanh(pre).reshape(row_count, blocks_here, 128) * hits[:, :, None]).astype(
        jnp.bfloat16
    )
    act_flat = act.reshape(row_count, lat_count)

    latent_block = first_block + jnp.arange(lat_count, dtype=jnp.int32) // 128
    keep = latent_block[None, :] < level_bounds[:, None]
    act_stack = jnp.where(keep[:, None, :], act_flat[None], jnp.zeros((), jnp.bfloat16))
    contrib = jnp.dot(
        act_stack.reshape(LEVELS * row_count, lat_count),
        dictionary,
        preferred_element_type=jnp.float32,
    ).reshape(LEVELS, row_count, half_width)
    levels = lat_sum(contrib, axis_names, n_lat, 0)

    errors = dec_bias[None, None, :] + levels - resid_full[None]
    squares = jnp.sum(errors * errors, axis=(1, 2))
    running = errors[LEVELS - 1]
    cum_list = [running]
    for level in range(LEVELS - 2, -1, -1):
        running = running + errors[level]
        cum_list.append(running)
    cum_err = jnp.stack(cum_list[::-1]).astype(jnp.bfloat16)

    level_of = jnp.sum((level_bounds[None, :] <= local_ids[:, None]).astype(jnp.int32), axis=1)
    err_half = jnp.take(cum_err, level_of, axis=0)
    partial_adjoint = jnp.einsum(
        "ktd,kcd->tkc", err_half, dict_blocks, preferred_element_type=jnp.float32
    )
    loss_rows = jnp.zeros((8, lat_count), jnp.float32).at[0, :LEVELS].set(squares)
    adjoint_rows = jnp.concatenate([partial_adjoint.reshape(row_count, lat_count), loss_rows], axis=0)
    summed_rows = axis_sum(adjoint_rows, axis_names, "wid", 2, 2)
    g_act = summed_rows[:row_count]
    loss_tile = jnp.zeros((8, 128), jnp.float32).at[0, :LEVELS].set(summed_rows[row_count, :LEVELS])
    total_sq = axis_sum(loss_tile, axis_names, "tok", lax.axis_size("tok"), 3)[0, :LEVELS]
    level_losses = total_sq / (row_count * lax.axis_size("tok") * half_width * lax.axis_size("wid"))
    mask_full = jnp.broadcast_to(hits[:, :, None], (row_count, blocks_here, 128)).reshape(
        row_count, lat_count
    )
    _, pull = jax.vjp(gelu_tanh, pre)
    g_pre = pull(g_act * mask_full)[0].astype(jnp.bfloat16)
    decode_term = jnp.einsum("ktd,tkc->dkc", err_half, act, preferred_element_type=jnp.float32)
    encode_term = lax.dot_general(
        resid, g_pre, (((0,), (0,)), ((), ())), preferred_element_type=jnp.float32
    )
    tok_count = lax.axis_size("tok")
    grad_share = ring_sum_scatter(
        (decode_term.reshape(half_width, lat_count) + encode_term).reshape(
            tok_count, half_width // tok_count, lat_count
        ),
        axis_names, "tok", tok_count, 4, jnp.bfloat16,
    )
    return (level_losses, grad_share)


def solution(mesh):
    axis_names = tuple(mesh.axis_names)
    n_lat = mesh.shape["lat"]
    return jax.shard_map(
        functools.partial(body, axis_names, n_lat),
        mesh=mesh,
        in_specs=(P("tok", "wid"), P("lat", "wid"), P("lat"), P("wid"), P("tok", None), P()),
        out_specs=(P(), P(("wid", "tok"), "lat")),
        check_vma=False,
    )
```

```python
import functools

import jax
import jax.numpy as jnp
from jax import lax
from jax.experimental import pallas as pl
from jax.experimental.pallas import tpu as pltpu
from jax.sharding import PartitionSpec as P

LEVELS = 4
MESH_ID = pl.DeviceIdType.MESH


def gelu_tanh(value):
    return jax.nn.gelu(value, approximate=True)


def device_on(axis_names, moved):
    return tuple(moved[n] if n in moved else lax.axis_index(n) for n in axis_names)


def remote(src, dst, send_sem, recv_sem, device):
    return pltpu.make_async_remote_copy(
        src_ref=src, dst_ref=dst, send_sem=send_sem, recv_sem=recv_sem,
        device_id=device, device_id_type=MESH_ID,
    )


def gather_phase(n, pos, dev_of, src_of, slot_of, send_sems, recv_sems):
    sends = []
    for d in range(1, n):
        c = (pos + d) % n
        cp = remote(src_of(c), slot_of(pos), send_sems.at[c], recv_sems.at[pos], dev_of(c))
        cp.start()
        sends.append(cp)
    slot_of(pos)[...] = src_of(pos)[...]
    for d in range(1, n):
        s = (pos + n - d) % n
        remote(src_of(s), slot_of(s), send_sems.at[s], recv_sems.at[s], dev_of(s)).wait_recv()
    return sends


def ring_reduce_scatter(n, pos, dev_of, src, recv, acc, sems, put):
    half = src.shape[1] // 2
    dirs = (1, n - 1)
    sends = []
    for s in range(n - 1):
        for h, dr in enumerate(dirs):
            k = (pos + (s + 1) * (n - dr)) % n
            source = src.at[k, pl.ds(h * half, half)] if s == 0 else acc.at[h, s - 1]
            cp = remote(source, recv.at[h, s], sems.at[h, 0, s], sems.at[h, 1, s], dev_of((pos + dr) % n))
            cp.start()
            sends.append(cp)
        for h, dr in enumerate(dirs):
            k2 = (pos + (s + 2) * (n - dr)) % n
            own = src.at[k2, pl.ds(h * half, half)]
            remote(own, recv.at[h, s], sems.at[h, 0, s], sems.at[h, 1, s],
                   dev_of((pos + n - dr) % n)).wait_recv()
            new = recv[h, s] + own[...]
            if s < n - 2:
                acc[h, s] = new
            else:
                put(h, new)
    return sends


def ring_all_gather(n, pos, dev_of, mine, dst, sems):
    half = mine.shape[0] // 2
    dirs = (1, n - 1)
    dst[pos] = mine[...]
    sends = []
    for s in range(n - 1):
        for h, dr in enumerate(dirs):
            k = (pos + s * (n - dr)) % n
            rows = pl.ds(h * half, half)
            source = mine.at[rows] if s == 0 else dst.at[k, rows]
            cp = remote(source, dst.at[k, rows], sems.at[h, 0, s], sems.at[h, 1, s], dev_of((pos + dr) % n))
            cp.start()
            sends.append(cp)
        for h, dr in enumerate(dirs):
            k2 = (pos + (s + 1) * (n - dr)) % n
            rows = pl.ds(h * half, half)
            remote(mine.at[rows], dst.at[k2, rows], sems.at[h, 0, s], sems.at[h, 1, s],
                   dev_of((pos + n - dr) % n)).wait_recv()
    return sends


def ring_sum_kernel(axis_names, axis, n, x_ref, out_ref, recv, acc, sems):
    me = lax.axis_index(axis)

    def dev_of(c):
        return device_on(axis_names, {axis: c})

    barrier = pltpu.get_barrier_semaphore()
    for d in range(1, n):
        pl.semaphore_signal(barrier, 1, device_id=dev_of((me + d) % n), device_id_type=MESH_ID)
    pl.semaphore_wait(barrier, n - 1)
    half = x_ref.shape[1] // 2

    def put(h, value):
        out_ref[pl.ds(h * half, half)] = value.astype(out_ref.dtype)

    sends = ring_reduce_scatter(n, me, dev_of, x_ref, recv, acc, sems, put)
    for cp in sends:
        cp.wait_send()


def ring_sum_scatter(x, axis_names, axis, n, cid, out_dtype):
    _, rows, width = x.shape
    return pl.pallas_call(
        functools.partial(ring_sum_kernel, axis_names, axis, n),
        out_shape=jax.ShapeDtypeStruct((rows, width), out_dtype),
        in_specs=[pl.BlockSpec(memory_space=pltpu.VMEM)],
        out_specs=pl.BlockSpec(memory_space=pltpu.VMEM),
        scratch_shapes=[
            pltpu.VMEM((2, n - 1, rows // 2, width), x.dtype),
            pltpu.VMEM((2, max(n - 2, 1), rows // 2, width), x.dtype),
            pltpu.SemaphoreType.DMA((2, 2, n - 1)),
        ],
        compiler_params=pltpu.CompilerParams(
            collective_id=cid, has_side_effects=True, vmem_limit_bytes=48 * 1024 * 1024
        ),
    )(x)


def axis_sum_kernel(axis_names, axis, n, x_ref, out_ref, slots, send_sem, recv_sem):
    me = lax.axis_index(axis)

    def dev_of(c):
        return device_on(axis_names, {axis: c})

    barrier = pltpu.get_barrier_semaphore()
    for d in range(1, n):
        pl.semaphore_signal(barrier, 1, device_id=dev_of((me + d) % n), device_id_type=MESH_ID)
    pl.semaphore_wait(barrier, n - 1)
    sends = gather_phase(n, me, dev_of, lambda c: x_ref, lambda c: slots.at[c], send_sem, recv_sem)
    total = slots[0]
    for s in range(1, n):
        total = total + slots[s]
    out_ref[...] = total
    for cp in sends:
        cp.wait_send()


def axis_sum(x, axis_names, axis, n, cid):
    return pl.pallas_call(
        functools.partial(axis_sum_kernel, axis_names, axis, n),
        out_shape=jax.ShapeDtypeStruct(x.shape, x.dtype),
        in_specs=[pl.BlockSpec(memory_space=pltpu.VMEM)],
        out_specs=pl.BlockSpec(memory_space=pltpu.VMEM),
        scratch_shapes=[
            pltpu.VMEM((n,) + x.shape, x.dtype),
            pltpu.SemaphoreType.DMA((n,)),
            pltpu.SemaphoreType.DMA((n,)),
        ],
        compiler_params=pltpu.CompilerParams(collective_id=cid, has_side_effects=True),
    )(x)


def ring_rs_steps(n, pos, dev_of, src, recv, acc, sems, put, sends):
    half = src.shape[1] // 2
    dirs = (1, n - 1)
    steps = []
    for s in range(n - 1):
        def start(s=s):
            for h, dr in enumerate(dirs):
                k = (pos + (s + 1) * (n - dr)) % n
                source = src.at[k, pl.ds(h * half, half)] if s == 0 else acc.at[h, s - 1]
                cp = remote(source, recv.at[h, s], sems.at[h, 0, s], sems.at[h, 1, s], dev_of((pos + dr) % n))
                cp.start()
                sends.append(cp)

        def finish(s=s):
            for h, dr in enumerate(dirs):
                k2 = (pos + (s + 2) * (n - dr)) % n
                own = src.at[k2, pl.ds(h * half, half)]
                remote(own, recv.at[h, s], sems.at[h, 0, s], sems.at[h, 1, s],
                       dev_of((pos + n - dr) % n)).wait_recv()
                new = recv[h, s] + own[...]
                if s < n - 2:
                    acc[h, s] = new
                else:
                    put(h, new)

        steps.append((start, finish))
    return steps


def ring_ag_steps(n, pos, dev_of, mine, dst, sems, sends):
    half = mine.shape[0] // 2
    dirs = (1, n - 1)
    steps = []
    for s in range(n - 1):
        def start(s=s):
            if s == 0:
                dst[pos] = mine[...]
            for h, dr in enumerate(dirs):
                k = (pos + s * (n - dr)) % n
                rows = pl.ds(h * half, half)
                source = mine.at[rows] if s == 0 else dst.at[k, rows]
                cp = remote(source, dst.at[k, rows], sems.at[h, 0, s], sems.at[h, 1, s], dev_of((pos + dr) % n))
                cp.start()
                sends.append(cp)

        def finish(s=s):
            for h, dr in enumerate(dirs):
                k2 = (pos + (s + 1) * (n - dr)) % n
                rows = pl.ds(h * half, half)
                remote(mine.at[rows], dst.at[k2, rows], sems.at[h, 0, s], sems.at[h, 1, s],
                       dev_of((pos + n - dr) % n)).wait_recv()

        steps.append((start, finish))
    return steps


def direct_step(n, pos, dev_of, src_of, slot_of, send_sems, recv_sems, sends, after):
    def start():
        for d in range(1, n):
            c = (pos + d) % n
            cp = remote(src_of(c), slot_of(pos), send_sems.at[c], recv_sems.at[pos], dev_of(c))
            cp.start()
            sends.append(cp)
        slot_of(pos)[...] = src_of(pos)[...]

    def finish():
        for d in range(1, n):
            s = (pos + n - d) % n
            remote(src_of(s), slot_of(s), send_sems.at[s], recv_sems.at[s], dev_of(s)).wait_recv()
        after()

    return [(start, finish)]


def lat_sum_kernel(axis_names, ny, nlo, nhi, x_ref, out_ref, recv1, acc1, part1, recv2, part2, recv3, part3,
                   ag2, ag1, ring_sems, sems):
    lat = lax.axis_index("lat")
    my_y = lat % ny
    my_z = lat // ny
    my_lo = my_z % nlo
    my_hi = my_z // nlo
    rows = x_ref.shape[1]
    cols = part1.shape[-1]
    c2 = rows // nlo
    c3 = c2 // nhi

    def y_dev(c):
        return device_on(axis_names, {"lat": my_z * ny + c})

    def lo_dev(c):
        return device_on(axis_names, {"lat": (my_hi * nlo + c) * ny + my_y})

    def hi_dev(c):
        return device_on(axis_names, {"lat": (c * nlo + my_lo) * ny + my_y})

    def rows_of(c, size):
        return pl.ds(pl.multiple_of(c * size, size), size)

    barrier = pltpu.get_barrier_semaphore()
    for n, pos, dev_of in ((ny, my_y, y_dev), (nlo, my_lo, lo_dev), (nhi, my_hi, hi_dev)):
        for d in range(1, n):
            pl.semaphore_signal(barrier, 1, device_id=dev_of((pos + d) % n), device_id_type=MESH_ID)
    pl.semaphore_wait(barrier, (ny - 1) + (nlo - 1) + (nhi - 1))

    def summed(slots, n):
        total = slots[0]
        for s in range(1, n):
            total = total + slots[s]
        return total

    sends = []
    streams = []
    for q in range(2):
        width = pl.ds(q * cols, cols)
        half = rows // 2

        def put(h, value, q=q, half=half):
            part1[q, pl.ds(h * half, half)] = value

        def sum_lo(q=q):
            part2[q] = summed(recv2.at[q], nlo)

        def sum_hi(q=q):
            part3[q] = summed(recv3.at[q], nhi)

        steps = []
        steps += ring_rs_steps(ny, my_y, y_dev, x_ref.at[:, :, width], recv1.at[q], acc1.at[q],
                               ring_sems.at[q, 0], put, sends)
        steps += direct_step(nlo, my_lo, lo_dev, lambda c, q=q: part1.at[q, rows_of(c, c2)],
                             lambda c, q=q: recv2.at[q, c], sems.at[q, 0, 0], sems.at[q, 0, 1], sends, sum_lo)
        steps += direct_step(nhi, my_hi, hi_dev, lambda c, q=q: part2.at[q, rows_of(c, c3)],
                             lambda c, q=q: recv3.at[q, c], sems.at[q, 1, 0], sems.at[q, 1, 1], sends, sum_hi)
        steps += direct_step(nhi, my_hi, hi_dev, lambda c, q=q: part3.at[q],
                             lambda c, q=q: ag2.at[q, rows_of(c, c3)], sems.at[q, 2, 0], sems.at[q, 2, 1],
                             sends, lambda: None)
        steps += direct_step(nlo, my_lo, lo_dev, lambda c, q=q: ag2.at[q],
                             lambda c, q=q: ag1.at[q, rows_of(c, c2)], sems.at[q, 3, 0], sems.at[q, 3, 1],
                             sends, lambda: None)
        steps += ring_ag_steps(ny, my_y, y_dev, ag1.at[q], out_ref.at[:, :, width], ring_sems.at[q, 1], sends)
        streams.append(steps)

    lag = ny - 1
    total_slots = len(streams[0]) + lag
    for slot in range(total_slots):
        active = []
        for q, offset in ((0, 0), (1, lag)):
            i = slot - offset
            if 0 <= i < len(streams[q]):
                active.append(streams[q][i])
        for start, _ in active:
            start()
        for _, finish in active:
            finish()
    for cp in sends:
        cp.wait_send()


def lat_sum(x, axis_names, n_lat, cid):
    ny = 4 if n_lat % 4 == 0 else 1
    nz = n_lat // ny
    nlo = 4 if nz % 4 == 0 else nz
    nhi = nz // nlo
    chunks, rows, width = x.shape
    assert chunks == ny and rows % (8 * nz) == 0 and width % 256 == 0
    cols = width // 2
    c2 = rows // nlo
    c3 = c2 // nhi
    f32 = jnp.float32
    most = max(nlo, nhi)
    return pl.pallas_call(
        functools.partial(lat_sum_kernel, axis_names, ny, nlo, nhi),
        out_shape=jax.ShapeDtypeStruct(x.shape, x.dtype),
        in_specs=[pl.BlockSpec(memory_space=pltpu.VMEM)],
        out_specs=pl.BlockSpec(memory_space=pltpu.VMEM),
        scratch_shapes=[
            pltpu.VMEM((2, 2, ny - 1, rows // 2, cols), f32),
            pltpu.VMEM((2, 2, max(ny - 2, 1), rows // 2, cols), f32),
            pltpu.VMEM((2, rows, cols), f32),
            pltpu.VMEM((2, nlo, c2, cols), f32),
            pltpu.VMEM((2, c2, cols), f32),
            pltpu.VMEM((2, nhi, c3, cols), f32),
            pltpu.VMEM((2, c3, cols), f32),
            pltpu.VMEM((2, c2, cols), f32),
            pltpu.VMEM((2, rows, cols), f32),
            pltpu.SemaphoreType.DMA((2, 2, 2, 2, ny - 1)),
            pltpu.SemaphoreType.DMA((2, 4, 2, most)),
        ],
        compiler_params=pltpu.CompilerParams(
            collective_id=cid, has_side_effects=True, vmem_limit_bytes=48 * 1024 * 1024
        ),
    )(x)


def body(axis_names, n_lat, resid, dictionary, enc_bias, dec_bias, active_blocks, level_bounds):
    row_count, half_width = resid.shape
    lat_count = dictionary.shape[0]
    blocks_here = lat_count // 128
    lat_position = lax.axis_index("lat")
    first_block = lat_position * blocks_here
    local_ids = first_block + jnp.arange(blocks_here, dtype=jnp.int32)
    resid_full = resid.astype(jnp.float32)
    dict_blocks = dictionary.reshape(blocks_here, 128, half_width)

    partial_pre = lax.dot_general(
        resid, dictionary, (((1,), (1,)), ((), ())), preferred_element_type=jnp.float32
    )
    pre = axis_sum(partial_pre, axis_names, "wid", 2, 1) + enc_bias[None, :]
    hits = jnp.any(active_blocks[:, :, None] == local_ids[None, None, :], axis=1).astype(
        jnp.float32
    )
    act = (gelu_tanh(pre).reshape(row_count, blocks_here, 128) * hits[:, :, None]).astype(
        jnp.bfloat16
    )
    act_flat = act.reshape(row_count, lat_count)

    latent_block = first_block + jnp.arange(lat_count, dtype=jnp.int32) // 128
    keep = latent_block[None, :] < level_bounds[:, None]
    act_stack = jnp.where(keep[:, None, :], act_flat[None], jnp.zeros((), jnp.bfloat16))
    contrib = jnp.dot(
        act_stack.reshape(LEVELS * row_count, lat_count),
        dictionary,
        preferred_element_type=jnp.float32,
    ).reshape(LEVELS, row_count, half_width)
    levels = lat_sum(contrib, axis_names, n_lat, 0)

    errors = dec_bias[None, None, :] + levels - resid_full[None]
    squares = jnp.sum(errors * errors, axis=(1, 2))
    running = errors[LEVELS - 1]
    cum_list = [running]
    for level in range(LEVELS - 2, -1, -1):
        running = running + errors[level]
        cum_list.append(running)
    cum_err = jnp.stack(cum_list[::-1]).astype(jnp.bfloat16)

    level_of = jnp.sum((level_bounds[None, :] <= local_ids[:, None]).astype(jnp.int32), axis=1)
    err_half = jnp.take(cum_err, level_of, axis=0)
    partial_adjoint = jnp.einsum(
        "ktd,kcd->tkc", err_half, dict_blocks, preferred_element_type=jnp.float32
    )
    loss_rows = jnp.zeros((8, lat_count), jnp.float32).at[0, :LEVELS].set(squares)
    adjoint_rows = jnp.concatenate([partial_adjoint.reshape(row_count, lat_count), loss_rows], axis=0)
    summed_rows = axis_sum(adjoint_rows, axis_names, "wid", 2, 2)
    g_act = summed_rows[:row_count]
    loss_tile = jnp.zeros((8, 128), jnp.float32).at[0, :LEVELS].set(summed_rows[row_count, :LEVELS])
    total_sq = axis_sum(loss_tile, axis_names, "tok", lax.axis_size("tok"), 3)[0, :LEVELS]
    level_losses = total_sq / (row_count * lax.axis_size("tok") * half_width * lax.axis_size("wid"))
    mask_full = jnp.broadcast_to(hits[:, :, None], (row_count, blocks_here, 128)).reshape(
        row_count, lat_count
    )
    _, pull = jax.vjp(gelu_tanh, pre)
    g_pre = pull(g_act * mask_full)[0].astype(jnp.bfloat16)
    decode_term = jnp.einsum("ktd,tkc->dkc", err_half, act, preferred_element_type=jnp.float32)
    encode_term = lax.dot_general(
        resid, g_pre, (((0,), (0,)), ((), ())), preferred_element_type=jnp.float32
    )
    tok_count = lax.axis_size("tok")
    grad_share = ring_sum_scatter(
        (decode_term.reshape(half_width, lat_count) + encode_term).reshape(
            tok_count, half_width // tok_count, lat_count
        ),
        axis_names, "tok", tok_count, 4, jnp.bfloat16,
    )
    return (level_losses, grad_share)


def solution(mesh):
    axis_names = tuple(mesh.axis_names)
    n_lat = mesh.shape["lat"]
    return jax.shard_map(
        functools.partial(body, axis_names, n_lat),
        mesh=mesh,
        in_specs=(P("tok", "wid"), P("lat", "wid"), P("lat"), P("wid"), P("tok", None), P()),
        out_specs=(P(), P(("wid", "tok"), "lat")),
        check_vma=False,
    )
```

```python
import functools

import jax
import jax.numpy as jnp
from jax import lax
from jax.experimental import pallas as pl
from jax.experimental.pallas import tpu as pltpu
from jax.sharding import PartitionSpec as P

LEVELS = 4
MESH_ID = pl.DeviceIdType.MESH


def gelu_tanh(value):
    return jax.nn.gelu(value, approximate=True)


def device_on(axis_names, moved):
    return tuple(moved[n] if n in moved else lax.axis_index(n) for n in axis_names)


def remote(src, dst, send_sem, recv_sem, device):
    return pltpu.make_async_remote_copy(
        src_ref=src, dst_ref=dst, send_sem=send_sem, recv_sem=recv_sem,
        device_id=device, device_id_type=MESH_ID,
    )


def gather_phase(n, pos, dev_of, src_of, slot_of, send_sems, recv_sems):
    sends = []
    for d in range(1, n):
        c = (pos + d) % n
        cp = remote(src_of(c), slot_of(pos), send_sems.at[c], recv_sems.at[pos], dev_of(c))
        cp.start()
        sends.append(cp)
    slot_of(pos)[...] = src_of(pos)[...]
    for d in range(1, n):
        s = (pos + n - d) % n
        remote(src_of(s), slot_of(s), send_sems.at[s], recv_sems.at[s], dev_of(s)).wait_recv()
    return sends


def ring_reduce_scatter(n, pos, dev_of, src, recv, acc, sems, put):
    half = src.shape[1] // 2
    dirs = (1, n - 1)
    sends = []
    for s in range(n - 1):
        for h, dr in enumerate(dirs):
            k = (pos + (s + 1) * (n - dr)) % n
            source = src.at[k, pl.ds(h * half, half)] if s == 0 else acc.at[h, s - 1]
            cp = remote(source, recv.at[h, s], sems.at[h, 0, s], sems.at[h, 1, s], dev_of((pos + dr) % n))
            cp.start()
            sends.append(cp)
        for h, dr in enumerate(dirs):
            k2 = (pos + (s + 2) * (n - dr)) % n
            own = src.at[k2, pl.ds(h * half, half)]
            remote(own, recv.at[h, s], sems.at[h, 0, s], sems.at[h, 1, s],
                   dev_of((pos + n - dr) % n)).wait_recv()
            new = recv[h, s] + own[...]
            if s < n - 2:
                acc[h, s] = new
            else:
                put(h, new)
    return sends


def ring_all_gather(n, pos, dev_of, mine, dst, sems):
    half = mine.shape[0] // 2
    dirs = (1, n - 1)
    dst[pos] = mine[...]
    sends = []
    for s in range(n - 1):
        for h, dr in enumerate(dirs):
            k = (pos + s * (n - dr)) % n
            rows = pl.ds(h * half, half)
            source = mine.at[rows] if s == 0 else dst.at[k, rows]
            cp = remote(source, dst.at[k, rows], sems.at[h, 0, s], sems.at[h, 1, s], dev_of((pos + dr) % n))
            cp.start()
            sends.append(cp)
        for h, dr in enumerate(dirs):
            k2 = (pos + (s + 1) * (n - dr)) % n
            rows = pl.ds(h * half, half)
            remote(mine.at[rows], dst.at[k2, rows], sems.at[h, 0, s], sems.at[h, 1, s],
                   dev_of((pos + n - dr) % n)).wait_recv()
    return sends


def grad_ring_kernel(axis_names, axis, n, lt_ref, rt_ref, loss_ref, out_ref, loss_out, part, recv, acc,
                     loss_slots, sems, loss_sems):
    me = lax.axis_index(axis)

    def dev_of(c):
        return device_on(axis_names, {axis: c})

    barrier = pltpu.get_barrier_semaphore()
    for d in range(1, n):
        pl.semaphore_signal(barrier, 1, device_id=dev_of((me + d) % n), device_id_type=MESH_ID)
    pl.semaphore_wait(barrier, n - 1)
    loss_sends = gather_phase(n, me, dev_of, lambda c: loss_ref, lambda c: loss_slots.at[c],
                              loss_sems.at[0], loss_sems.at[1])
    blocks, width, _ = lt_ref.shape
    rows = width // n
    lane = rt_ref.shape[2]
    for c in range(n):
        for k in range(blocks):
            part[c, :, pl.ds(k * lane, lane)] = jnp.dot(
                lt_ref[k, pl.ds(c * rows, rows), :], rt_ref[k], preferred_element_type=jnp.float32
            )
    half = rows // 2

    def put(h, value):
        out_ref[pl.ds(h * half, half)] = value.astype(out_ref.dtype)

    sends = ring_reduce_scatter(n, me, dev_of, part, recv, acc, sems, put)
    total = loss_slots[0]
    for s in range(1, n):
        total = total + loss_slots[s]
    loss_out[...] = total
    for cp in sends + loss_sends:
        cp.wait_send()


def grad_ring(lt, rt, loss_tile, axis_names, axis, n, cid):
    blocks, width, _ = lt.shape
    lane = rt.shape[2]
    rows = width // n
    cols = blocks * lane
    f32 = jnp.float32
    return pl.pallas_call(
        functools.partial(grad_ring_kernel, axis_names, axis, n),
        out_shape=(jax.ShapeDtypeStruct((rows, cols), jnp.bfloat16),
                   jax.ShapeDtypeStruct(loss_tile.shape, f32)),
        in_specs=[pl.BlockSpec(memory_space=pltpu.VMEM)] * 3,
        out_specs=(pl.BlockSpec(memory_space=pltpu.VMEM), pl.BlockSpec(memory_space=pltpu.VMEM)),
        scratch_shapes=[
            pltpu.VMEM((n, rows, cols), f32),
            pltpu.VMEM((2, n - 1, rows // 2, cols), f32),
            pltpu.VMEM((2, max(n - 2, 1), rows // 2, cols), f32),
            pltpu.VMEM((n,) + loss_tile.shape, f32),
            pltpu.SemaphoreType.DMA((2, 2, n - 1)),
            pltpu.SemaphoreType.DMA((2, n)),
        ],
        compiler_params=pltpu.CompilerParams(
            collective_id=cid, has_side_effects=True, vmem_limit_bytes=56 * 1024 * 1024
        ),
    )(lt, rt, loss_tile)


def axis_sum_kernel(axis_names, axis, n, x_ref, out_ref, slots, send_sem, recv_sem):
    me = lax.axis_index(axis)

    def dev_of(c):
        return device_on(axis_names, {axis: c})

    barrier = pltpu.get_barrier_semaphore()
    for d in range(1, n):
        pl.semaphore_signal(barrier, 1, device_id=dev_of((me + d) % n), device_id_type=MESH_ID)
    pl.semaphore_wait(barrier, n - 1)
    sends = gather_phase(n, me, dev_of, lambda c: x_ref, lambda c: slots.at[c], send_sem, recv_sem)
    total = slots[0]
    for s in range(1, n):
        total = total + slots[s]
    out_ref[...] = total
    for cp in sends:
        cp.wait_send()


def axis_sum(x, axis_names, axis, n, cid):
    return pl.pallas_call(
        functools.partial(axis_sum_kernel, axis_names, axis, n),
        out_shape=jax.ShapeDtypeStruct(x.shape, x.dtype),
        in_specs=[pl.BlockSpec(memory_space=pltpu.VMEM)],
        out_specs=pl.BlockSpec(memory_space=pltpu.VMEM),
        scratch_shapes=[
            pltpu.VMEM((n,) + x.shape, x.dtype),
            pltpu.SemaphoreType.DMA((n,)),
            pltpu.SemaphoreType.DMA((n,)),
        ],
        compiler_params=pltpu.CompilerParams(collective_id=cid, has_side_effects=True),
    )(x)


def ring_rs_steps(n, pos, dev_of, src, recv, acc, sems, put, sends):
    half = src.shape[1] // 2
    dirs = (1, n - 1)
    steps = []
    for s in range(n - 1):
        def start(s=s):
            for h, dr in enumerate(dirs):
                k = (pos + (s + 1) * (n - dr)) % n
                source = src.at[k, pl.ds(h * half, half)] if s == 0 else acc.at[h, s - 1]
                cp = remote(source, recv.at[h, s], sems.at[h, 0, s], sems.at[h, 1, s], dev_of((pos + dr) % n))
                cp.start()
                sends.append(cp)

        def finish(s=s):
            for h, dr in enumerate(dirs):
                k2 = (pos + (s + 2) * (n - dr)) % n
                own = src.at[k2, pl.ds(h * half, half)]
                remote(own, recv.at[h, s], sems.at[h, 0, s], sems.at[h, 1, s],
                       dev_of((pos + n - dr) % n)).wait_recv()
                new = recv[h, s] + own[...]
                if s < n - 2:
                    acc[h, s] = new
                else:
                    put(h, new)

        steps.append((start, finish))
    return steps


def ring_ag_steps(n, pos, dev_of, mine, dst, sems, sends):
    half = mine.shape[0] // 2
    dirs = (1, n - 1)
    steps = []
    for s in range(n - 1):
        def start(s=s):
            if s == 0:
                dst[pos] = mine[...]
            for h, dr in enumerate(dirs):
                k = (pos + s * (n - dr)) % n
                rows = pl.ds(h * half, half)
                source = mine.at[rows] if s == 0 else dst.at[k, rows]
                cp = remote(source, dst.at[k, rows], sems.at[h, 0, s], sems.at[h, 1, s], dev_of((pos + dr) % n))
                cp.start()
                sends.append(cp)

        def finish(s=s):
            for h, dr in enumerate(dirs):
                k2 = (pos + (s + 1) * (n - dr)) % n
                rows = pl.ds(h * half, half)
                remote(mine.at[rows], dst.at[k2, rows], sems.at[h, 0, s], sems.at[h, 1, s],
                       dev_of((pos + n - dr) % n)).wait_recv()

        steps.append((start, finish))
    return steps


def direct_step(n, pos, dev_of, src_of, slot_of, send_sems, recv_sems, sends, after):
    def start():
        for d in range(1, n):
            c = (pos + d) % n
            cp = remote(src_of(c), slot_of(pos), send_sems.at[c], recv_sems.at[pos], dev_of(c))
            cp.start()
            sends.append(cp)
        slot_of(pos)[...] = src_of(pos)[...]

    def finish():
        for d in range(1, n):
            s = (pos + n - d) % n
            remote(src_of(s), slot_of(s), send_sems.at[s], recv_sems.at[s], dev_of(s)).wait_recv()
        after()

    return [(start, finish)]


def lat_sum_kernel(axis_names, ny, nlo, nhi, x_ref, out_ref, recv1, acc1, part1, recv2, part2, recv3, part3,
                   ag2, ag1, ring_sems, sems):
    lat = lax.axis_index("lat")
    my_y = lat % ny
    my_z = lat // ny
    my_lo = my_z % nlo
    my_hi = my_z // nlo
    rows = x_ref.shape[1]
    cols = part1.shape[-1]
    c2 = rows // nlo
    c3 = c2 // nhi

    def y_dev(c):
        return device_on(axis_names, {"lat": my_z * ny + c})

    def lo_dev(c):
        return device_on(axis_names, {"lat": (my_hi * nlo + c) * ny + my_y})

    def hi_dev(c):
        return device_on(axis_names, {"lat": (c * nlo + my_lo) * ny + my_y})

    def rows_of(c, size):
        return pl.ds(pl.multiple_of(c * size, size), size)

    barrier = pltpu.get_barrier_semaphore()
    for n, pos, dev_of in ((ny, my_y, y_dev), (nlo, my_lo, lo_dev), (nhi, my_hi, hi_dev)):
        for d in range(1, n):
            pl.semaphore_signal(barrier, 1, device_id=dev_of((pos + d) % n), device_id_type=MESH_ID)
    pl.semaphore_wait(barrier, (ny - 1) + (nlo - 1) + (nhi - 1))

    def summed(slots, n):
        total = slots[0]
        for s in range(1, n):
            total = total + slots[s]
        return total

    sends = []
    streams = []
    for q in range(2):
        width = pl.ds(q * cols, cols)
        half = rows // 2

        def put(h, value, q=q, half=half):
            part1[q, pl.ds(h * half, half)] = value

        def sum_lo(q=q):
            part2[q] = summed(recv2.at[q], nlo)

        def sum_hi(q=q):
            part3[q] = summed(recv3.at[q], nhi)

        steps = []
        steps += ring_rs_steps(ny, my_y, y_dev, x_ref.at[:, :, width], recv1.at[q], acc1.at[q],
                               ring_sems.at[q, 0], put, sends)
        steps += direct_step(nlo, my_lo, lo_dev, lambda c, q=q: part1.at[q, rows_of(c, c2)],
                             lambda c, q=q: recv2.at[q, c], sems.at[q, 0, 0], sems.at[q, 0, 1], sends, sum_lo)
        steps += direct_step(nhi, my_hi, hi_dev, lambda c, q=q: part2.at[q, rows_of(c, c3)],
                             lambda c, q=q: recv3.at[q, c], sems.at[q, 1, 0], sems.at[q, 1, 1], sends, sum_hi)
        steps += direct_step(nhi, my_hi, hi_dev, lambda c, q=q: part3.at[q],
                             lambda c, q=q: ag2.at[q, rows_of(c, c3)], sems.at[q, 2, 0], sems.at[q, 2, 1],
                             sends, lambda: None)
        steps += direct_step(nlo, my_lo, lo_dev, lambda c, q=q: ag2.at[q],
                             lambda c, q=q: ag1.at[q, rows_of(c, c2)], sems.at[q, 3, 0], sems.at[q, 3, 1],
                             sends, lambda: None)
        steps += ring_ag_steps(ny, my_y, y_dev, ag1.at[q], out_ref.at[:, :, width], ring_sems.at[q, 1], sends)
        streams.append(steps)

    lag = ny - 1
    total_slots = len(streams[0]) + lag
    for slot in range(total_slots):
        active = []
        for q, offset in ((0, 0), (1, lag)):
            i = slot - offset
            if 0 <= i < len(streams[q]):
                active.append(streams[q][i])
        for start, _ in active:
            start()
        for _, finish in active:
            finish()
    for cp in sends:
        cp.wait_send()


def lat_sum(x, axis_names, n_lat, cid):
    ny = 4 if n_lat % 4 == 0 else 1
    nz = n_lat // ny
    nlo = 4 if nz % 4 == 0 else nz
    nhi = nz // nlo
    chunks, rows, width = x.shape
    assert chunks == ny and rows % (8 * nz) == 0 and width % 256 == 0
    cols = width // 2
    c2 = rows // nlo
    c3 = c2 // nhi
    f32 = jnp.float32
    most = max(nlo, nhi)
    return pl.pallas_call(
        functools.partial(lat_sum_kernel, axis_names, ny, nlo, nhi),
        out_shape=jax.ShapeDtypeStruct(x.shape, x.dtype),
        in_specs=[pl.BlockSpec(memory_space=pltpu.VMEM)],
        out_specs=pl.BlockSpec(memory_space=pltpu.VMEM),
        scratch_shapes=[
            pltpu.VMEM((2, 2, ny - 1, rows // 2, cols), f32),
            pltpu.VMEM((2, 2, max(ny - 2, 1), rows // 2, cols), f32),
            pltpu.VMEM((2, rows, cols), f32),
            pltpu.VMEM((2, nlo, c2, cols), f32),
            pltpu.VMEM((2, c2, cols), f32),
            pltpu.VMEM((2, nhi, c3, cols), f32),
            pltpu.VMEM((2, c3, cols), f32),
            pltpu.VMEM((2, c2, cols), f32),
            pltpu.VMEM((2, rows, cols), f32),
            pltpu.SemaphoreType.DMA((2, 2, 2, 2, ny - 1)),
            pltpu.SemaphoreType.DMA((2, 4, 2, most)),
        ],
        compiler_params=pltpu.CompilerParams(
            collective_id=cid, has_side_effects=True, vmem_limit_bytes=48 * 1024 * 1024
        ),
    )(x)


def body(axis_names, n_lat, resid, dictionary, enc_bias, dec_bias, active_blocks, level_bounds):
    row_count, half_width = resid.shape
    lat_count = dictionary.shape[0]
    blocks_here = lat_count // 128
    lat_position = lax.axis_index("lat")
    first_block = lat_position * blocks_here
    local_ids = first_block + jnp.arange(blocks_here, dtype=jnp.int32)
    resid_full = resid.astype(jnp.float32)
    dict_blocks = dictionary.reshape(blocks_here, 128, half_width)

    partial_pre = lax.dot_general(
        resid, dictionary, (((1,), (1,)), ((), ())), preferred_element_type=jnp.float32
    )
    pre = axis_sum(partial_pre, axis_names, "wid", 2, 1) + enc_bias[None, :]
    hits = jnp.any(active_blocks[:, :, None] == local_ids[None, None, :], axis=1).astype(
        jnp.float32
    )
    act = (gelu_tanh(pre).reshape(row_count, blocks_here, 128) * hits[:, :, None]).astype(
        jnp.bfloat16
    )
    act_flat = act.reshape(row_count, lat_count)

    latent_block = first_block + jnp.arange(lat_count, dtype=jnp.int32) // 128
    keep = latent_block[None, :] < level_bounds[:, None]
    act_stack = jnp.where(keep[:, None, :], act_flat[None], jnp.zeros((), jnp.bfloat16))
    contrib = jnp.dot(
        act_stack.reshape(LEVELS * row_count, lat_count),
        dictionary,
        preferred_element_type=jnp.float32,
    ).reshape(LEVELS, row_count, half_width)
    levels = lat_sum(contrib, axis_names, n_lat, 0)

    errors = dec_bias[None, None, :] + levels - resid_full[None]
    squares = jnp.sum(errors * errors, axis=(1, 2))
    running = errors[LEVELS - 1]
    cum_list = [running]
    for level in range(LEVELS - 2, -1, -1):
        running = running + errors[level]
        cum_list.append(running)
    cum_err = jnp.stack(cum_list[::-1]).astype(jnp.bfloat16)

    level_of = jnp.sum((level_bounds[None, :] <= local_ids[:, None]).astype(jnp.int32), axis=1)
    err_half = jnp.take(cum_err, level_of, axis=0)
    partial_adjoint = jnp.einsum(
        "ktd,kcd->tkc", err_half, dict_blocks, preferred_element_type=jnp.float32
    )
    loss_rows = jnp.zeros((8, lat_count), jnp.float32).at[0, :LEVELS].set(squares)
    adjoint_rows = jnp.concatenate([partial_adjoint.reshape(row_count, lat_count), loss_rows], axis=0)
    summed_rows = axis_sum(adjoint_rows, axis_names, "wid", 2, 2)
    g_act = summed_rows[:row_count]
    loss_tile = jnp.zeros((8, 128), jnp.float32).at[0, :LEVELS].set(summed_rows[row_count, :LEVELS])
    mask_full = jnp.broadcast_to(hits[:, :, None], (row_count, blocks_here, 128)).reshape(
        row_count, lat_count
    )
    _, pull = jax.vjp(gelu_tanh, pre)
    g_pre = pull(g_act * mask_full)[0].astype(jnp.bfloat16)
    left = jnp.concatenate(
        [err_half, jnp.broadcast_to(resid[None], (blocks_here, row_count, half_width))], axis=1
    )
    lt = jnp.transpose(left, (0, 2, 1))
    right = jnp.concatenate(
        [act.reshape(row_count, blocks_here, 128), g_pre.reshape(row_count, blocks_here, 128)], axis=0
    )
    rt = jnp.transpose(right, (1, 0, 2))
    tok_count = lax.axis_size("tok")
    grad_share, loss_sum = grad_ring(lt, rt, loss_tile, axis_names, "tok", tok_count, 4)
    total_sq = loss_sum[0, :LEVELS]
    level_losses = total_sq / (row_count * tok_count * half_width * lax.axis_size("wid"))
    return (level_losses, grad_share)


def solution(mesh):
    axis_names = tuple(mesh.axis_names)
    n_lat = mesh.shape["lat"]
    return jax.shard_map(
        functools.partial(body, axis_names, n_lat),
        mesh=mesh,
        in_specs=(P("tok", "wid"), P("lat", "wid"), P("lat"), P("wid"), P("tok", None), P()),
        out_specs=(P(), P(("wid", "tok"), "lat")),
        check_vma=False,
    )
```

```python
import functools

import jax
import jax.numpy as jnp
from jax import lax
from jax.experimental import pallas as pl
from jax.experimental.pallas import tpu as pltpu
from jax.sharding import PartitionSpec as P

LEVELS = 4
MESH_ID = pl.DeviceIdType.MESH


def gelu_tanh(value):
    return jax.nn.gelu(value, approximate=True)


def device_on(axis_names, moved):
    return tuple(moved[n] if n in moved else lax.axis_index(n) for n in axis_names)


def remote(src, dst, send_sem, recv_sem, device):
    return pltpu.make_async_remote_copy(
        src_ref=src, dst_ref=dst, send_sem=send_sem, recv_sem=recv_sem,
        device_id=device, device_id_type=MESH_ID,
    )


def gather_phase(n, pos, dev_of, src_of, slot_of, send_sems, recv_sems):
    sends = []
    for d in range(1, n):
        c = (pos + d) % n
        cp = remote(src_of(c), slot_of(pos), send_sems.at[c], recv_sems.at[pos], dev_of(c))
        cp.start()
        sends.append(cp)
    slot_of(pos)[...] = src_of(pos)[...]
    for d in range(1, n):
        s = (pos + n - d) % n
        remote(src_of(s), slot_of(s), send_sems.at[s], recv_sems.at[s], dev_of(s)).wait_recv()
    return sends


def ring_reduce_scatter(n, pos, dev_of, src, recv, acc, sems, put):
    half = src.shape[1] // 2
    dirs = (1, n - 1)
    sends = []
    for s in range(n - 1):
        for h, dr in enumerate(dirs):
            k = (pos + (s + 1) * (n - dr)) % n
            source = src.at[k, pl.ds(h * half, half)] if s == 0 else acc.at[h, s - 1]
            cp = remote(source, recv.at[h, s], sems.at[h, 0, s], sems.at[h, 1, s], dev_of((pos + dr) % n))
            cp.start()
            sends.append(cp)
        for h, dr in enumerate(dirs):
            k2 = (pos + (s + 2) * (n - dr)) % n
            own = src.at[k2, pl.ds(h * half, half)]
            remote(own, recv.at[h, s], sems.at[h, 0, s], sems.at[h, 1, s],
                   dev_of((pos + n - dr) % n)).wait_recv()
            new = recv[h, s] + own[...]
            if s < n - 2:
                acc[h, s] = new
            else:
                put(h, new)
    return sends


def ring_all_gather(n, pos, dev_of, mine, dst, sems):
    half = mine.shape[0] // 2
    dirs = (1, n - 1)
    dst[pos] = mine[...]
    sends = []
    for s in range(n - 1):
        for h, dr in enumerate(dirs):
            k = (pos + s * (n - dr)) % n
            rows = pl.ds(h * half, half)
            source = mine.at[rows] if s == 0 else dst.at[k, rows]
            cp = remote(source, dst.at[k, rows], sems.at[h, 0, s], sems.at[h, 1, s], dev_of((pos + dr) % n))
            cp.start()
            sends.append(cp)
        for h, dr in enumerate(dirs):
            k2 = (pos + (s + 1) * (n - dr)) % n
            rows = pl.ds(h * half, half)
            remote(mine.at[rows], dst.at[k2, rows], sems.at[h, 0, s], sems.at[h, 1, s],
                   dev_of((pos + n - dr) % n)).wait_recv()
    return sends


def grad_ring_kernel(axis_names, axis, n, lt_ref, rt_ref, loss_ref, out_ref, loss_out, part, recv, acc,
                     loss_slots, sems, loss_sems):
    me = lax.axis_index(axis)

    def dev_of(c):
        return device_on(axis_names, {axis: c})

    barrier = pltpu.get_barrier_semaphore()
    for d in range(1, n):
        pl.semaphore_signal(barrier, 1, device_id=dev_of((me + d) % n), device_id_type=MESH_ID)
    pl.semaphore_wait(barrier, n - 1)
    loss_sends = gather_phase(n, me, dev_of, lambda c: loss_ref, lambda c: loss_slots.at[c],
                              loss_sems.at[0], loss_sems.at[1])
    blocks, width, _ = lt_ref.shape
    rows = width // n
    lane = rt_ref.shape[2]

    def make_chunk(c):
        for k in range(blocks):
            part[c, :, pl.ds(k * lane, lane)] = jnp.dot(
                lt_ref[k, pl.ds(pl.multiple_of(c * rows, rows), rows), :], rt_ref[k],
                preferred_element_type=jnp.float32,
            )

    first = sorted({(n - 1) % n, 1 % n})
    later = [o for o in dict.fromkeys((2 % n, 0)) if o not in first]
    for o in first:
        make_chunk((me + o) % n)
    half = rows // 2

    def put(h, value):
        out_ref[pl.ds(h * half, half)] = value.astype(out_ref.dtype)

    sends = []
    steps = ring_rs_steps(n, me, dev_of, part, recv, acc, sems, put, sends)
    for i, (start, finish) in enumerate(steps):
        start()
        if i == 0:
            for o in later:
                make_chunk((me + o) % n)
        finish()
    total = loss_slots[0]
    for s in range(1, n):
        total = total + loss_slots[s]
    loss_out[...] = total
    for cp in sends + loss_sends:
        cp.wait_send()


def grad_ring(lt, rt, loss_tile, axis_names, axis, n, cid):
    blocks, width, _ = lt.shape
    lane = rt.shape[2]
    rows = width // n
    cols = blocks * lane
    f32 = jnp.float32
    return pl.pallas_call(
        functools.partial(grad_ring_kernel, axis_names, axis, n),
        out_shape=(jax.ShapeDtypeStruct((rows, cols), jnp.bfloat16),
                   jax.ShapeDtypeStruct(loss_tile.shape, f32)),
        in_specs=[pl.BlockSpec(memory_space=pltpu.VMEM)] * 3,
        out_specs=(pl.BlockSpec(memory_space=pltpu.VMEM), pl.BlockSpec(memory_space=pltpu.VMEM)),
        scratch_shapes=[
            pltpu.VMEM((n, rows, cols), f32),
            pltpu.VMEM((2, n - 1, rows // 2, cols), f32),
            pltpu.VMEM((2, max(n - 2, 1), rows // 2, cols), f32),
            pltpu.VMEM((n,) + loss_tile.shape, f32),
            pltpu.SemaphoreType.DMA((2, 2, n - 1)),
            pltpu.SemaphoreType.DMA((2, n)),
        ],
        compiler_params=pltpu.CompilerParams(
            collective_id=cid, has_side_effects=True, vmem_limit_bytes=56 * 1024 * 1024
        ),
    )(lt, rt, loss_tile)


def axis_sum_kernel(axis_names, axis, n, x_ref, out_ref, slots, send_sem, recv_sem):
    me = lax.axis_index(axis)

    def dev_of(c):
        return device_on(axis_names, {axis: c})

    barrier = pltpu.get_barrier_semaphore()
    for d in range(1, n):
        pl.semaphore_signal(barrier, 1, device_id=dev_of((me + d) % n), device_id_type=MESH_ID)
    pl.semaphore_wait(barrier, n - 1)
    sends = gather_phase(n, me, dev_of, lambda c: x_ref, lambda c: slots.at[c], send_sem, recv_sem)
    total = slots[0]
    for s in range(1, n):
        total = total + slots[s]
    out_ref[...] = total
    for cp in sends:
        cp.wait_send()


def axis_sum(x, axis_names, axis, n, cid):
    return pl.pallas_call(
        functools.partial(axis_sum_kernel, axis_names, axis, n),
        out_shape=jax.ShapeDtypeStruct(x.shape, x.dtype),
        in_specs=[pl.BlockSpec(memory_space=pltpu.VMEM)],
        out_specs=pl.BlockSpec(memory_space=pltpu.VMEM),
        scratch_shapes=[
            pltpu.VMEM((n,) + x.shape, x.dtype),
            pltpu.SemaphoreType.DMA((n,)),
            pltpu.SemaphoreType.DMA((n,)),
        ],
        compiler_params=pltpu.CompilerParams(collective_id=cid, has_side_effects=True),
    )(x)


def ring_rs_steps(n, pos, dev_of, src, recv, acc, sems, put, sends):
    half = src.shape[1] // 2
    dirs = (1, n - 1)
    steps = []
    for s in range(n - 1):
        def start(s=s):
            for h, dr in enumerate(dirs):
                k = (pos + (s + 1) * (n - dr)) % n
                source = src.at[k, pl.ds(h * half, half)] if s == 0 else acc.at[h, s - 1]
                cp = remote(source, recv.at[h, s], sems.at[h, 0, s], sems.at[h, 1, s], dev_of((pos + dr) % n))
                cp.start()
                sends.append(cp)

        def finish(s=s):
            for h, dr in enumerate(dirs):
                k2 = (pos + (s + 2) * (n - dr)) % n
                own = src.at[k2, pl.ds(h * half, half)]
                remote(own, recv.at[h, s], sems.at[h, 0, s], sems.at[h, 1, s],
                       dev_of((pos + n - dr) % n)).wait_recv()
                new = recv[h, s] + own[...]
                if s < n - 2:
                    acc[h, s] = new
                else:
                    put(h, new)

        steps.append((start, finish))
    return steps


def ring_ag_steps(n, pos, dev_of, mine, dst, sems, sends):
    half = mine.shape[0] // 2
    dirs = (1, n - 1)
    steps = []
    for s in range(n - 1):
        def start(s=s):
            if s == 0:
                dst[pos] = mine[...]
            for h, dr in enumerate(dirs):
                k = (pos + s * (n - dr)) % n
                rows = pl.ds(h * half, half)
                source = mine.at[rows] if s == 0 else dst.at[k, rows]
                cp = remote(source, dst.at[k, rows], sems.at[h, 0, s], sems.at[h, 1, s], dev_of((pos + dr) % n))
                cp.start()
                sends.append(cp)

        def finish(s=s):
            for h, dr in enumerate(dirs):
                k2 = (pos + (s + 1) * (n - dr)) % n
                rows = pl.ds(h * half, half)
                remote(mine.at[rows], dst.at[k2, rows], sems.at[h, 0, s], sems.at[h, 1, s],
                       dev_of((pos + n - dr) % n)).wait_recv()

        steps.append((start, finish))
    return steps


def direct_step(n, pos, dev_of, src_of, slot_of, send_sems, recv_sems, sends, after):
    def start():
        for d in range(1, n):
            c = (pos + d) % n
            cp = remote(src_of(c), slot_of(pos), send_sems.at[c], recv_sems.at[pos], dev_of(c))
            cp.start()
            sends.append(cp)
        slot_of(pos)[...] = src_of(pos)[...]

    def finish():
        for d in range(1, n):
            s = (pos + n - d) % n
            remote(src_of(s), slot_of(s), send_sems.at[s], recv_sems.at[s], dev_of(s)).wait_recv()
        after()

    return [(start, finish)]


def lat_sum_kernel(axis_names, ny, nlo, nhi, x_ref, out_ref, recv1, acc1, part1, recv2, part2, recv3, part3,
                   ag2, ag1, ring_sems, sems):
    lat = lax.axis_index("lat")
    my_y = lat % ny
    my_z = lat // ny
    my_lo = my_z % nlo
    my_hi = my_z // nlo
    rows = x_ref.shape[1]
    cols = part1.shape[-1]
    c2 = rows // nlo
    c3 = c2 // nhi

    def y_dev(c):
        return device_on(axis_names, {"lat": my_z * ny + c})

    def lo_dev(c):
        return device_on(axis_names, {"lat": (my_hi * nlo + c) * ny + my_y})

    def hi_dev(c):
        return device_on(axis_names, {"lat": (c * nlo + my_lo) * ny + my_y})

    def rows_of(c, size):
        return pl.ds(pl.multiple_of(c * size, size), size)

    barrier = pltpu.get_barrier_semaphore()
    for n, pos, dev_of in ((ny, my_y, y_dev), (nlo, my_lo, lo_dev), (nhi, my_hi, hi_dev)):
        for d in range(1, n):
            pl.semaphore_signal(barrier, 1, device_id=dev_of((pos + d) % n), device_id_type=MESH_ID)
    pl.semaphore_wait(barrier, (ny - 1) + (nlo - 1) + (nhi - 1))

    def summed(slots, n):
        total = slots[0]
        for s in range(1, n):
            total = total + slots[s]
        return total

    sends = []
    streams = []
    for q in range(2):
        width = pl.ds(q * cols, cols)
        half = rows // 2

        def put(h, value, q=q, half=half):
            part1[q, pl.ds(h * half, half)] = value

        def sum_lo(q=q):
            part2[q] = summed(recv2.at[q], nlo)

        def sum_hi(q=q):
            part3[q] = summed(recv3.at[q], nhi)

        steps = []
        steps += ring_rs_steps(ny, my_y, y_dev, x_ref.at[:, :, width], recv1.at[q], acc1.at[q],
                               ring_sems.at[q, 0], put, sends)
        steps += direct_step(nlo, my_lo, lo_dev, lambda c, q=q: part1.at[q, rows_of(c, c2)],
                             lambda c, q=q: recv2.at[q, c], sems.at[q, 0, 0], sems.at[q, 0, 1], sends, sum_lo)
        steps += direct_step(nhi, my_hi, hi_dev, lambda c, q=q: part2.at[q, rows_of(c, c3)],
                             lambda c, q=q: recv3.at[q, c], sems.at[q, 1, 0], sems.at[q, 1, 1], sends, sum_hi)
        steps += direct_step(nhi, my_hi, hi_dev, lambda c, q=q: part3.at[q],
                             lambda c, q=q: ag2.at[q, rows_of(c, c3)], sems.at[q, 2, 0], sems.at[q, 2, 1],
                             sends, lambda: None)
        steps += direct_step(nlo, my_lo, lo_dev, lambda c, q=q: ag2.at[q],
                             lambda c, q=q: ag1.at[q, rows_of(c, c2)], sems.at[q, 3, 0], sems.at[q, 3, 1],
                             sends, lambda: None)
        steps += ring_ag_steps(ny, my_y, y_dev, ag1.at[q], out_ref.at[:, :, width], ring_sems.at[q, 1], sends)
        streams.append(steps)

    lag = ny - 1
    total_slots = len(streams[0]) + lag
    for slot in range(total_slots):
        active = []
        for q, offset in ((0, 0), (1, lag)):
            i = slot - offset
            if 0 <= i < len(streams[q]):
                active.append(streams[q][i])
        for start, _ in active:
            start()
        for _, finish in active:
            finish()
    for cp in sends:
        cp.wait_send()


def lat_sum(x, axis_names, n_lat, cid):
    ny = 4 if n_lat % 4 == 0 else 1
    nz = n_lat // ny
    nlo = 4 if nz % 4 == 0 else nz
    nhi = nz // nlo
    chunks, rows, width = x.shape
    assert chunks == ny and rows % (8 * nz) == 0 and width % 256 == 0
    cols = width // 2
    c2 = rows // nlo
    c3 = c2 // nhi
    f32 = jnp.float32
    most = max(nlo, nhi)
    return pl.pallas_call(
        functools.partial(lat_sum_kernel, axis_names, ny, nlo, nhi),
        out_shape=jax.ShapeDtypeStruct(x.shape, x.dtype),
        in_specs=[pl.BlockSpec(memory_space=pltpu.VMEM)],
        out_specs=pl.BlockSpec(memory_space=pltpu.VMEM),
        scratch_shapes=[
            pltpu.VMEM((2, 2, ny - 1, rows // 2, cols), f32),
            pltpu.VMEM((2, 2, max(ny - 2, 1), rows // 2, cols), f32),
            pltpu.VMEM((2, rows, cols), f32),
            pltpu.VMEM((2, nlo, c2, cols), f32),
            pltpu.VMEM((2, c2, cols), f32),
            pltpu.VMEM((2, nhi, c3, cols), f32),
            pltpu.VMEM((2, c3, cols), f32),
            pltpu.VMEM((2, c2, cols), f32),
            pltpu.VMEM((2, rows, cols), f32),
            pltpu.SemaphoreType.DMA((2, 2, 2, 2, ny - 1)),
            pltpu.SemaphoreType.DMA((2, 4, 2, most)),
        ],
        compiler_params=pltpu.CompilerParams(
            collective_id=cid, has_side_effects=True, vmem_limit_bytes=48 * 1024 * 1024
        ),
    )(x)


def body(axis_names, n_lat, resid, dictionary, enc_bias, dec_bias, active_blocks, level_bounds):
    row_count, half_width = resid.shape
    lat_count = dictionary.shape[0]
    blocks_here = lat_count // 128
    lat_position = lax.axis_index("lat")
    first_block = lat_position * blocks_here
    local_ids = first_block + jnp.arange(blocks_here, dtype=jnp.int32)
    resid_full = resid.astype(jnp.float32)
    dict_blocks = dictionary.reshape(blocks_here, 128, half_width)

    partial_pre = lax.dot_general(
        resid, dictionary, (((1,), (1,)), ((), ())), preferred_element_type=jnp.float32
    )
    pre = axis_sum(partial_pre, axis_names, "wid", 2, 1) + enc_bias[None, :]
    hits = jnp.any(active_blocks[:, :, None] == local_ids[None, None, :], axis=1).astype(
        jnp.float32
    )
    act = (gelu_tanh(pre).reshape(row_count, blocks_here, 128) * hits[:, :, None]).astype(
        jnp.bfloat16
    )
    act_flat = act.reshape(row_count, lat_count)

    latent_block = first_block + jnp.arange(lat_count, dtype=jnp.int32) // 128
    keep = latent_block[None, :] < level_bounds[:, None]
    act_stack = jnp.where(keep[:, None, :], act_flat[None], jnp.zeros((), jnp.bfloat16))
    contrib = jnp.dot(
        act_stack.reshape(LEVELS * row_count, lat_count),
        dictionary,
        preferred_element_type=jnp.float32,
    ).reshape(LEVELS, row_count, half_width)
    levels = lat_sum(contrib, axis_names, n_lat, 0)

    errors = dec_bias[None, None, :] + levels - resid_full[None]
    squares = jnp.sum(errors * errors, axis=(1, 2))
    level_of = jnp.sum((level_bounds[None, :] <= local_ids[:, None]).astype(jnp.int32), axis=1)
    running = jnp.broadcast_to(errors[LEVELS - 1][None], (blocks_here, row_count, half_width))
    for level in range(LEVELS - 2, -1, -1):
        used = (level >= level_of).astype(jnp.float32)[:, None, None]
        running = running + used * errors[level][None]
    err_half = running.astype(jnp.bfloat16)
    partial_adjoint = jnp.einsum(
        "ktd,kcd->tkc", err_half, dict_blocks, preferred_element_type=jnp.float32
    )
    loss_rows = jnp.zeros((8, lat_count), jnp.float32).at[0, :LEVELS].set(squares)
    adjoint_rows = jnp.concatenate([partial_adjoint.reshape(row_count, lat_count), loss_rows], axis=0)
    summed_rows = axis_sum(adjoint_rows, axis_names, "wid", 2, 2)
    g_act = summed_rows[:row_count]
    loss_tile = jnp.zeros((8, 128), jnp.float32).at[0, :LEVELS].set(summed_rows[row_count, :LEVELS])
    mask_full = jnp.broadcast_to(hits[:, :, None], (row_count, blocks_here, 128)).reshape(
        row_count, lat_count
    )
    _, pull = jax.vjp(gelu_tanh, pre)
    g_pre = pull(g_act * mask_full)[0].astype(jnp.bfloat16)
    left = jnp.concatenate(
        [err_half, jnp.broadcast_to(resid[None], (blocks_here, row_count, half_width))], axis=1
    )
    lt = jnp.transpose(left, (0, 2, 1))
    right = jnp.concatenate(
        [act.reshape(row_count, blocks_here, 128), g_pre.reshape(row_count, blocks_here, 128)], axis=0
    )
    rt = jnp.transpose(right, (1, 0, 2))
    tok_count = lax.axis_size("tok")
    grad_share, loss_sum = grad_ring(lt, rt, loss_tile, axis_names, "tok", tok_count, 4)
    total_sq = loss_sum[0, :LEVELS]
    level_losses = total_sq / (row_count * tok_count * half_width * lax.axis_size("wid"))
    return (level_losses, grad_share)


def solution(mesh):
    axis_names = tuple(mesh.axis_names)
    n_lat = mesh.shape["lat"]
    return jax.shard_map(
        functools.partial(body, axis_names, n_lat),
        mesh=mesh,
        in_specs=(P("tok", "wid"), P("lat", "wid"), P("lat"), P("wid"), P("tok", None), P()),
        out_specs=(P(), P(("wid", "tok"), "lat")),
        check_vma=False,
    )
```

```python
import functools

import jax
import jax.numpy as jnp
from jax import lax
from jax.experimental import pallas as pl
from jax.experimental.pallas import tpu as pltpu
from jax.sharding import PartitionSpec as P

LEVELS = 4
MESH_ID = pl.DeviceIdType.MESH


def gelu_tanh(value):
    return jax.nn.gelu(value, approximate=True)


def device_on(axis_names, moved):
    return tuple(moved[n] if n in moved else lax.axis_index(n) for n in axis_names)


def remote(src, dst, send_sem, recv_sem, device):
    return pltpu.make_async_remote_copy(
        src_ref=src, dst_ref=dst, send_sem=send_sem, recv_sem=recv_sem,
        device_id=device, device_id_type=MESH_ID,
    )


def gather_phase(n, pos, dev_of, src_of, slot_of, send_sems, recv_sems):
    sends = []
    for d in range(1, n):
        c = (pos + d) % n
        cp = remote(src_of(c), slot_of(pos), send_sems.at[c], recv_sems.at[pos], dev_of(c))
        cp.start()
        sends.append(cp)
    slot_of(pos)[...] = src_of(pos)[...]
    for d in range(1, n):
        s = (pos + n - d) % n
        remote(src_of(s), slot_of(s), send_sems.at[s], recv_sems.at[s], dev_of(s)).wait_recv()
    return sends


def ring_reduce_scatter(n, pos, dev_of, src, recv, acc, sems, put):
    half = src.shape[1] // 2
    dirs = (1, n - 1)
    sends = []
    for s in range(n - 1):
        for h, dr in enumerate(dirs):
            k = (pos + (s + 1) * (n - dr)) % n
            source = src.at[k, pl.ds(h * half, half)] if s == 0 else acc.at[h, s - 1]
            cp = remote(source, recv.at[h, s], sems.at[h, 0, s], sems.at[h, 1, s], dev_of((pos + dr) % n))
            cp.start()
            sends.append(cp)
        for h, dr in enumerate(dirs):
            k2 = (pos + (s + 2) * (n - dr)) % n
            own = src.at[k2, pl.ds(h * half, half)]
            remote(own, recv.at[h, s], sems.at[h, 0, s], sems.at[h, 1, s],
                   dev_of((pos + n - dr) % n)).wait_recv()
            new = recv[h, s] + own[...]
            if s < n - 2:
                acc[h, s] = new
            else:
                put(h, new)
    return sends


def ring_all_gather(n, pos, dev_of, mine, dst, sems):
    half = mine.shape[0] // 2
    dirs = (1, n - 1)
    dst[pos] = mine[...]
    sends = []
    for s in range(n - 1):
        for h, dr in enumerate(dirs):
            k = (pos + s * (n - dr)) % n
            rows = pl.ds(h * half, half)
            source = mine.at[rows] if s == 0 else dst.at[k, rows]
            cp = remote(source, dst.at[k, rows], sems.at[h, 0, s], sems.at[h, 1, s], dev_of((pos + dr) % n))
            cp.start()
            sends.append(cp)
        for h, dr in enumerate(dirs):
            k2 = (pos + (s + 1) * (n - dr)) % n
            rows = pl.ds(h * half, half)
            remote(mine.at[rows], dst.at[k2, rows], sems.at[h, 0, s], sems.at[h, 1, s],
                   dev_of((pos + n - dr) % n)).wait_recv()
    return sends


def grad_ring_kernel(axis_names, axis, n, lt_ref, rt_ref, loss_ref, out_ref, loss_out, part, recv, acc,
                     loss_slots, sems, loss_sems):
    me = lax.axis_index(axis)

    def dev_of(c):
        return device_on(axis_names, {axis: c})

    barrier = pltpu.get_barrier_semaphore()
    for d in range(1, n):
        pl.semaphore_signal(barrier, 1, device_id=dev_of((me + d) % n), device_id_type=MESH_ID)
    pl.semaphore_wait(barrier, n - 1)
    loss_sends = gather_phase(n, me, dev_of, lambda c: loss_ref, lambda c: loss_slots.at[c],
                              loss_sems.at[0], loss_sems.at[1])
    blocks, width, _ = lt_ref.shape
    rows = width // n
    lane = rt_ref.shape[2]

    def make_chunk(c):
        for k in range(blocks):
            part[c, :, pl.ds(k * lane, lane)] = jnp.dot(
                lt_ref[k, pl.ds(pl.multiple_of(c * rows, rows), rows), :], rt_ref[k],
                preferred_element_type=jnp.float32,
            )

    first = sorted({(n - 1) % n, 1 % n})
    later = [o for o in dict.fromkeys((2 % n, 0)) if o not in first]
    for o in first:
        make_chunk((me + o) % n)
    half = rows // 2

    def put(h, value):
        out_ref[pl.ds(h * half, half)] = value.astype(out_ref.dtype)

    sends = []
    steps = ring_rs_steps(n, me, dev_of, part, recv, acc, sems, put, sends)
    for i, (start, finish) in enumerate(steps):
        start()
        if i == 0:
            for o in later:
                make_chunk((me + o) % n)
        finish()
    total = loss_slots[0]
    for s in range(1, n):
        total = total + loss_slots[s]
    loss_out[...] = total
    for cp in sends + loss_sends:
        cp.wait_send()


def grad_ring(lt, rt, loss_tile, axis_names, axis, n, cid):
    blocks, width, _ = lt.shape
    lane = rt.shape[2]
    rows = width // n
    cols = blocks * lane
    f32 = jnp.float32
    return pl.pallas_call(
        functools.partial(grad_ring_kernel, axis_names, axis, n),
        out_shape=(jax.ShapeDtypeStruct((rows, cols), jnp.bfloat16),
                   jax.ShapeDtypeStruct(loss_tile.shape, f32)),
        in_specs=[pl.BlockSpec(memory_space=pltpu.VMEM)] * 3,
        out_specs=(pl.BlockSpec(memory_space=pltpu.VMEM), pl.BlockSpec(memory_space=pltpu.VMEM)),
        scratch_shapes=[
            pltpu.VMEM((n, rows, cols), f32),
            pltpu.VMEM((2, n - 1, rows // 2, cols), f32),
            pltpu.VMEM((2, max(n - 2, 1), rows // 2, cols), f32),
            pltpu.VMEM((n,) + loss_tile.shape, f32),
            pltpu.SemaphoreType.DMA((2, 2, n - 1)),
            pltpu.SemaphoreType.DMA((2, n)),
        ],
        compiler_params=pltpu.CompilerParams(
            collective_id=cid, has_side_effects=True, vmem_limit_bytes=56 * 1024 * 1024
        ),
    )(lt, rt, loss_tile)


def axis_sum_kernel(axis_names, axis, n, x_ref, out_ref, slots, send_sem, recv_sem):
    me = lax.axis_index(axis)

    def dev_of(c):
        return device_on(axis_names, {axis: c})

    barrier = pltpu.get_barrier_semaphore()
    for d in range(1, n):
        pl.semaphore_signal(barrier, 1, device_id=dev_of((me + d) % n), device_id_type=MESH_ID)
    pl.semaphore_wait(barrier, n - 1)
    sends = gather_phase(n, me, dev_of, lambda c: x_ref, lambda c: slots.at[c], send_sem, recv_sem)
    total = slots[0]
    for s in range(1, n):
        total = total + slots[s]
    out_ref[...] = total
    for cp in sends:
        cp.wait_send()


def axis_sum(x, axis_names, axis, n, cid):
    return pl.pallas_call(
        functools.partial(axis_sum_kernel, axis_names, axis, n),
        out_shape=jax.ShapeDtypeStruct(x.shape, x.dtype),
        in_specs=[pl.BlockSpec(memory_space=pltpu.VMEM)],
        out_specs=pl.BlockSpec(memory_space=pltpu.VMEM),
        scratch_shapes=[
            pltpu.VMEM((n,) + x.shape, x.dtype),
            pltpu.SemaphoreType.DMA((n,)),
            pltpu.SemaphoreType.DMA((n,)),
        ],
        compiler_params=pltpu.CompilerParams(collective_id=cid, has_side_effects=True),
    )(x)


def ring_rs_steps(n, pos, dev_of, src, recv, acc, sems, put, sends):
    half = src.shape[1] // 2
    dirs = (1, n - 1)
    steps = []
    for s in range(n - 1):
        def start(s=s):
            for h, dr in enumerate(dirs):
                k = (pos + (s + 1) * (n - dr)) % n
                source = src.at[k, pl.ds(h * half, half)] if s == 0 else acc.at[h, s - 1]
                cp = remote(source, recv.at[h, s], sems.at[h, 0, s], sems.at[h, 1, s], dev_of((pos + dr) % n))
                cp.start()
                sends.append(cp)

        def finish(s=s):
            for h, dr in enumerate(dirs):
                k2 = (pos + (s + 2) * (n - dr)) % n
                own = src.at[k2, pl.ds(h * half, half)]
                remote(own, recv.at[h, s], sems.at[h, 0, s], sems.at[h, 1, s],
                       dev_of((pos + n - dr) % n)).wait_recv()
                new = recv[h, s] + own[...]
                if s < n - 2:
                    acc[h, s] = new
                else:
                    put(h, new)

        steps.append((start, finish))
    return steps


def ring_ag_steps(n, pos, dev_of, mine, dst, sems, sends):
    half = mine.shape[0] // 2
    dirs = (1, n - 1)
    steps = []
    for s in range(n - 1):
        def start(s=s):
            if s == 0:
                dst[pos] = mine[...]
            for h, dr in enumerate(dirs):
                k = (pos + s * (n - dr)) % n
                rows = pl.ds(h * half, half)
                source = mine.at[rows] if s == 0 else dst.at[k, rows]
                cp = remote(source, dst.at[k, rows], sems.at[h, 0, s], sems.at[h, 1, s], dev_of((pos + dr) % n))
                cp.start()
                sends.append(cp)

        def finish(s=s):
            for h, dr in enumerate(dirs):
                k2 = (pos + (s + 1) * (n - dr)) % n
                rows = pl.ds(h * half, half)
                remote(mine.at[rows], dst.at[k2, rows], sems.at[h, 0, s], sems.at[h, 1, s],
                       dev_of((pos + n - dr) % n)).wait_recv()

        steps.append((start, finish))
    return steps


def direct_step(n, pos, dev_of, src_of, slot_of, send_sems, recv_sems, sends, after):
    def start():
        for d in range(1, n):
            c = (pos + d) % n
            cp = remote(src_of(c), slot_of(pos), send_sems.at[c], recv_sems.at[pos], dev_of(c))
            cp.start()
            sends.append(cp)
        slot_of(pos)[...] = src_of(pos)[...]

    def finish():
        for d in range(1, n):
            s = (pos + n - d) % n
            remote(src_of(s), slot_of(s), send_sems.at[s], recv_sems.at[s], dev_of(s)).wait_recv()
        after()

    return [(start, finish)]


def lat_sum_kernel(axis_names, ny, nlo, nhi, x_ref, out_ref, recv1, acc1, part1, recv2, part2, recv3, part3,
                   ag2, ag1, ring_sems, sems):
    lat = lax.axis_index("lat")
    my_y = lat % ny
    my_z = lat // ny
    my_lo = my_z % nlo
    my_hi = my_z // nlo
    rows = x_ref.shape[1]
    cols = part1.shape[-1]
    c2 = rows // nlo
    c3 = c2 // nhi

    def y_dev(c):
        return device_on(axis_names, {"lat": my_z * ny + c})

    def lo_dev(c):
        return device_on(axis_names, {"lat": (my_hi * nlo + c) * ny + my_y})

    def hi_dev(c):
        return device_on(axis_names, {"lat": (c * nlo + my_lo) * ny + my_y})

    def rows_of(c, size):
        return pl.ds(pl.multiple_of(c * size, size), size)

    barrier = pltpu.get_barrier_semaphore()
    for n, pos, dev_of in ((ny, my_y, y_dev), (nlo, my_lo, lo_dev), (nhi, my_hi, hi_dev)):
        for d in range(1, n):
            pl.semaphore_signal(barrier, 1, device_id=dev_of((pos + d) % n), device_id_type=MESH_ID)
    pl.semaphore_wait(barrier, (ny - 1) + (nlo - 1) + (nhi - 1))

    def summed(slots, n):
        total = slots[0]
        for s in range(1, n):
            total = total + slots[s]
        return total

    sends = []
    streams = []
    for q in range(2):
        width = pl.ds(q * cols, cols)
        half = rows // 2

        def put(h, value, q=q, half=half):
            part1[q, pl.ds(h * half, half)] = value

        def sum_lo(q=q):
            part2[q] = summed(recv2.at[q], nlo)

        def sum_hi(q=q):
            part3[q] = summed(recv3.at[q], nhi)

        steps = []
        steps += ring_rs_steps(ny, my_y, y_dev, x_ref.at[:, :, width], recv1.at[q], acc1.at[q],
                               ring_sems.at[q, 0], put, sends)
        steps += direct_step(nlo, my_lo, lo_dev, lambda c, q=q: part1.at[q, rows_of(c, c2)],
                             lambda c, q=q: recv2.at[q, c], sems.at[q, 0, 0], sems.at[q, 0, 1], sends, sum_lo)
        steps += direct_step(nhi, my_hi, hi_dev, lambda c, q=q: part2.at[q, rows_of(c, c3)],
                             lambda c, q=q: recv3.at[q, c], sems.at[q, 1, 0], sems.at[q, 1, 1], sends, sum_hi)
        steps += direct_step(nhi, my_hi, hi_dev, lambda c, q=q: part3.at[q],
                             lambda c, q=q: ag2.at[q, rows_of(c, c3)], sems.at[q, 2, 0], sems.at[q, 2, 1],
                             sends, lambda: None)
        steps += direct_step(nlo, my_lo, lo_dev, lambda c, q=q: ag2.at[q],
                             lambda c, q=q: ag1.at[q, rows_of(c, c2)], sems.at[q, 3, 0], sems.at[q, 3, 1],
                             sends, lambda: None)
        steps += ring_ag_steps(ny, my_y, y_dev, ag1.at[q], out_ref.at[:, :, width], ring_sems.at[q, 1], sends)
        streams.append(steps)

    lag = ny - 1
    total_slots = len(streams[0]) + lag
    for slot in range(total_slots):
        active = []
        for q, offset in ((0, 0), (1, lag)):
            i = slot - offset
            if 0 <= i < len(streams[q]):
                active.append(streams[q][i])
        for start, _ in active:
            start()
        for _, finish in active:
            finish()
    for cp in sends:
        cp.wait_send()


def lat_sum(x, axis_names, n_lat, cid):
    ny = 4 if n_lat % 4 == 0 else 1
    nz = n_lat // ny
    nlo = 4 if nz % 4 == 0 else nz
    nhi = nz // nlo
    chunks, rows, width = x.shape
    assert chunks == ny and rows % (8 * nz) == 0 and width % 256 == 0
    cols = width // 2
    c2 = rows // nlo
    c3 = c2 // nhi
    f32 = jnp.float32
    most = max(nlo, nhi)
    return pl.pallas_call(
        functools.partial(lat_sum_kernel, axis_names, ny, nlo, nhi),
        out_shape=jax.ShapeDtypeStruct(x.shape, x.dtype),
        in_specs=[pl.BlockSpec(memory_space=pltpu.VMEM)],
        out_specs=pl.BlockSpec(memory_space=pltpu.VMEM),
        scratch_shapes=[
            pltpu.VMEM((2, 2, ny - 1, rows // 2, cols), f32),
            pltpu.VMEM((2, 2, max(ny - 2, 1), rows // 2, cols), f32),
            pltpu.VMEM((2, rows, cols), f32),
            pltpu.VMEM((2, nlo, c2, cols), f32),
            pltpu.VMEM((2, c2, cols), f32),
            pltpu.VMEM((2, nhi, c3, cols), f32),
            pltpu.VMEM((2, c3, cols), f32),
            pltpu.VMEM((2, c2, cols), f32),
            pltpu.VMEM((2, rows, cols), f32),
            pltpu.SemaphoreType.DMA((2, 2, 2, 2, ny - 1)),
            pltpu.SemaphoreType.DMA((2, 4, 2, most)),
        ],
        compiler_params=pltpu.CompilerParams(
            collective_id=cid, has_side_effects=True, vmem_limit_bytes=48 * 1024 * 1024
        ),
    )(x)


def body(axis_names, n_lat, resid, dictionary, enc_bias, dec_bias, active_blocks, level_bounds):
    row_count, half_width = resid.shape
    lat_count = dictionary.shape[0]
    blocks_here = lat_count // 128
    lat_position = lax.axis_index("lat")
    first_block = lat_position * blocks_here
    local_ids = first_block + jnp.arange(blocks_here, dtype=jnp.int32)
    resid_full = resid.astype(jnp.float32)
    dict_blocks = dictionary.reshape(blocks_here, 128, half_width)

    partial_pre = lax.dot_general(
        resid, dictionary, (((1,), (1,)), ((), ())), preferred_element_type=jnp.float32
    )
    pre = axis_sum(partial_pre, axis_names, "wid", 2, 1) + enc_bias[None, :]
    hits = jnp.any(active_blocks[:, :, None] == local_ids[None, None, :], axis=1).astype(
        jnp.float32
    )
    act = (gelu_tanh(pre).reshape(row_count, blocks_here, 128) * hits[:, :, None]).astype(
        jnp.bfloat16
    )
    act_flat = act.reshape(row_count, lat_count)

    latent_block = first_block + jnp.arange(lat_count, dtype=jnp.int32) // 128
    keep = latent_block[None, :] < level_bounds[:, None]
    act_stack = jnp.where(keep[:, None, :], act_flat[None], jnp.zeros((), jnp.bfloat16))
    contrib = jnp.dot(
        act_stack.reshape(LEVELS * row_count, lat_count),
        dictionary,
        preferred_element_type=jnp.float32,
    ).reshape(LEVELS, row_count, half_width)
    levels = lat_sum(contrib, axis_names, n_lat, 0)

    errors = dec_bias[None, None, :] + levels - resid_full[None]
    squares = jnp.sum(errors * errors, axis=(1, 2))
    running = errors[LEVELS - 1]
    cum_list = [running]
    for level in range(LEVELS - 2, -1, -1):
        running = running + errors[level]
        cum_list.append(running)
    cum_err = jnp.stack(cum_list[::-1]).astype(jnp.bfloat16)

    level_of = jnp.sum((level_bounds[None, :] <= local_ids[:, None]).astype(jnp.int32), axis=1)
    err_half = jnp.take(cum_err, level_of, axis=0)
    partial_adjoint = jnp.einsum(
        "ktd,kcd->tkc", err_half, dict_blocks, preferred_element_type=jnp.float32
    )
    loss_rows = jnp.zeros((8, lat_count), jnp.float32).at[0, :LEVELS].set(squares)
    adjoint_rows = jnp.concatenate([partial_adjoint.reshape(row_count, lat_count), loss_rows], axis=0)
    summed_rows = axis_sum(adjoint_rows, axis_names, "wid", 2, 2)
    g_act = summed_rows[:row_count]
    loss_tile = jnp.zeros((8, 128), jnp.float32).at[0, :LEVELS].set(summed_rows[row_count, :LEVELS])
    mask_full = jnp.broadcast_to(hits[:, :, None], (row_count, blocks_here, 128)).reshape(
        row_count, lat_count
    )
    _, pull = jax.vjp(gelu_tanh, pre)
    g_pre = pull(g_act * mask_full)[0].astype(jnp.bfloat16)
    left = jnp.concatenate(
        [err_half, jnp.broadcast_to(resid[None], (blocks_here, row_count, half_width))], axis=1
    )
    lt = jnp.transpose(left, (0, 2, 1))
    right = jnp.concatenate(
        [act.reshape(row_count, blocks_here, 128), g_pre.reshape(row_count, blocks_here, 128)], axis=0
    )
    rt = jnp.transpose(right, (1, 0, 2))
    tok_count = lax.axis_size("tok")
    grad_share, loss_sum = grad_ring(lt, rt, loss_tile, axis_names, "tok", tok_count, 4)
    total_sq = loss_sum[0, :LEVELS]
    level_losses = total_sq / (row_count * tok_count * half_width * lax.axis_size("wid"))
    return (level_losses, grad_share)


def solution(mesh):
    axis_names = tuple(mesh.axis_names)
    n_lat = mesh.shape["lat"]
    return jax.shard_map(
        functools.partial(body, axis_names, n_lat),
        mesh=mesh,
        in_specs=(P("tok", "wid"), P("lat", "wid"), P("lat"), P("wid"), P("tok", None), P()),
        out_specs=(P(), P(("wid", "tok"), "lat")),
        check_vma=False,
    )
```

```python
import functools

import jax
import jax.numpy as jnp
from jax import lax
from jax.experimental import pallas as pl
from jax.experimental.pallas import tpu as pltpu
from jax.sharding import PartitionSpec as P

LEVELS = 4
MESH_ID = pl.DeviceIdType.MESH


def gelu_tanh(value):
    return jax.nn.gelu(value, approximate=True)


def device_on(axis_names, moved):
    return tuple(moved[n] if n in moved else lax.axis_index(n) for n in axis_names)


def remote(src, dst, send_sem, recv_sem, device):
    return pltpu.make_async_remote_copy(
        src_ref=src, dst_ref=dst, send_sem=send_sem, recv_sem=recv_sem,
        device_id=device, device_id_type=MESH_ID,
    )


def gather_phase(n, pos, dev_of, src_of, slot_of, send_sems, recv_sems):
    sends = []
    for d in range(1, n):
        c = (pos + d) % n
        cp = remote(src_of(c), slot_of(pos), send_sems.at[c], recv_sems.at[pos], dev_of(c))
        cp.start()
        sends.append(cp)
    slot_of(pos)[...] = src_of(pos)[...]
    for d in range(1, n):
        s = (pos + n - d) % n
        remote(src_of(s), slot_of(s), send_sems.at[s], recv_sems.at[s], dev_of(s)).wait_recv()
    return sends


def ring_reduce_scatter(n, pos, dev_of, src, recv, acc, sems, put):
    half = src.shape[1] // 2
    dirs = (1, n - 1)
    sends = []
    for s in range(n - 1):
        for h, dr in enumerate(dirs):
            k = (pos + (s + 1) * (n - dr)) % n
            source = src.at[k, pl.ds(h * half, half)] if s == 0 else acc.at[h, s - 1]
            cp = remote(source, recv.at[h, s], sems.at[h, 0, s], sems.at[h, 1, s], dev_of((pos + dr) % n))
            cp.start()
            sends.append(cp)
        for h, dr in enumerate(dirs):
            k2 = (pos + (s + 2) * (n - dr)) % n
            own = src.at[k2, pl.ds(h * half, half)]
            remote(own, recv.at[h, s], sems.at[h, 0, s], sems.at[h, 1, s],
                   dev_of((pos + n - dr) % n)).wait_recv()
            new = recv[h, s] + own[...]
            if s < n - 2:
                acc[h, s] = new
            else:
                put(h, new)
    return sends


def ring_all_gather(n, pos, dev_of, mine, dst, sems):
    half = mine.shape[0] // 2
    dirs = (1, n - 1)
    dst[pos] = mine[...]
    sends = []
    for s in range(n - 1):
        for h, dr in enumerate(dirs):
            k = (pos + s * (n - dr)) % n
            rows = pl.ds(h * half, half)
            source = mine.at[rows] if s == 0 else dst.at[k, rows]
            cp = remote(source, dst.at[k, rows], sems.at[h, 0, s], sems.at[h, 1, s], dev_of((pos + dr) % n))
            cp.start()
            sends.append(cp)
        for h, dr in enumerate(dirs):
            k2 = (pos + (s + 1) * (n - dr)) % n
            rows = pl.ds(h * half, half)
            remote(mine.at[rows], dst.at[k2, rows], sems.at[h, 0, s], sems.at[h, 1, s],
                   dev_of((pos + n - dr) % n)).wait_recv()
    return sends


def grad_ring_kernel(axis_names, axis, n, lt_ref, rt_ref, loss_ref, out_ref, loss_out, part, recv, acc,
                     loss_slots, sems, loss_sems):
    me = lax.axis_index(axis)

    def dev_of(c):
        return device_on(axis_names, {axis: c})

    barrier = pltpu.get_barrier_semaphore()
    for d in range(1, n):
        pl.semaphore_signal(barrier, 1, device_id=dev_of((me + d) % n), device_id_type=MESH_ID)
    pl.semaphore_wait(barrier, n - 1)
    loss_sends = gather_phase(n, me, dev_of, lambda c: loss_ref, lambda c: loss_slots.at[c],
                              loss_sems.at[0], loss_sems.at[1])
    blocks, width, _ = lt_ref.shape
    rows = width // n
    lane = rt_ref.shape[2]

    def make_chunk(c):
        for k in range(blocks):
            part[c, :, pl.ds(k * lane, lane)] = jnp.dot(
                lt_ref[k, pl.ds(pl.multiple_of(c * rows, rows), rows), :], rt_ref[k],
                preferred_element_type=jnp.float32,
            )

    first = sorted({(n - 1) % n, 1 % n})
    later = [o for o in dict.fromkeys((2 % n, 0)) if o not in first]
    for o in first:
        make_chunk((me + o) % n)
    half = rows // 2

    def put(h, value):
        out_ref[pl.ds(h * half, half)] = value.astype(out_ref.dtype)

    sends = []
    steps = ring_rs_steps(n, me, dev_of, part, recv, acc, sems, put, sends)
    for i, (start, finish) in enumerate(steps):
        start()
        if i == 0:
            for o in later:
                make_chunk((me + o) % n)
        finish()
    total = loss_slots[0]
    for s in range(1, n):
        total = total + loss_slots[s]
    loss_out[...] = total
    for cp in sends + loss_sends:
        cp.wait_send()


def grad_ring(lt, rt, loss_tile, axis_names, axis, n, cid):
    blocks, width, _ = lt.shape
    lane = rt.shape[2]
    rows = width // n
    cols = blocks * lane
    f32 = jnp.float32
    return pl.pallas_call(
        functools.partial(grad_ring_kernel, axis_names, axis, n),
        out_shape=(jax.ShapeDtypeStruct((rows, cols), jnp.bfloat16),
                   jax.ShapeDtypeStruct(loss_tile.shape, f32)),
        in_specs=[pl.BlockSpec(memory_space=pltpu.VMEM)] * 3,
        out_specs=(pl.BlockSpec(memory_space=pltpu.VMEM), pl.BlockSpec(memory_space=pltpu.VMEM)),
        scratch_shapes=[
            pltpu.VMEM((n, rows, cols), f32),
            pltpu.VMEM((2, n - 1, rows // 2, cols), f32),
            pltpu.VMEM((2, max(n - 2, 1), rows // 2, cols), f32),
            pltpu.VMEM((n,) + loss_tile.shape, f32),
            pltpu.SemaphoreType.DMA((2, 2, n - 1)),
            pltpu.SemaphoreType.DMA((2, n)),
        ],
        compiler_params=pltpu.CompilerParams(
            collective_id=cid, has_side_effects=True, vmem_limit_bytes=56 * 1024 * 1024
        ),
    )(lt, rt, loss_tile)


def axis_sum_kernel(axis_names, axis, n, x_ref, out_ref, slots, send_sem, recv_sem):
    me = lax.axis_index(axis)

    def dev_of(c):
        return device_on(axis_names, {axis: c})

    barrier = pltpu.get_barrier_semaphore()
    for d in range(1, n):
        pl.semaphore_signal(barrier, 1, device_id=dev_of((me + d) % n), device_id_type=MESH_ID)
    pl.semaphore_wait(barrier, n - 1)
    sends = gather_phase(n, me, dev_of, lambda c: x_ref, lambda c: slots.at[c], send_sem, recv_sem)
    total = slots[0]
    for s in range(1, n):
        total = total + slots[s]
    out_ref[...] = total
    for cp in sends:
        cp.wait_send()


def axis_sum(x, axis_names, axis, n, cid):
    return pl.pallas_call(
        functools.partial(axis_sum_kernel, axis_names, axis, n),
        out_shape=jax.ShapeDtypeStruct(x.shape, x.dtype),
        in_specs=[pl.BlockSpec(memory_space=pltpu.VMEM)],
        out_specs=pl.BlockSpec(memory_space=pltpu.VMEM),
        scratch_shapes=[
            pltpu.VMEM((n,) + x.shape, x.dtype),
            pltpu.SemaphoreType.DMA((n,)),
            pltpu.SemaphoreType.DMA((n,)),
        ],
        compiler_params=pltpu.CompilerParams(collective_id=cid, has_side_effects=True),
    )(x)


def ring_rs_steps(n, pos, dev_of, src, recv, acc, sems, put, sends):
    half = src.shape[1] // 2
    dirs = (1, n - 1)
    steps = []
    for s in range(n - 1):
        def start(s=s):
            for h, dr in enumerate(dirs):
                k = (pos + (s + 1) * (n - dr)) % n
                source = src.at[k, pl.ds(h * half, half)] if s == 0 else acc.at[h, s - 1]
                cp = remote(source, recv.at[h, s], sems.at[h, 0, s], sems.at[h, 1, s], dev_of((pos + dr) % n))
                cp.start()
                sends.append(cp)

        def finish(s=s):
            for h, dr in enumerate(dirs):
                k2 = (pos + (s + 2) * (n - dr)) % n
                own = src.at[k2, pl.ds(h * half, half)]
                remote(own, recv.at[h, s], sems.at[h, 0, s], sems.at[h, 1, s],
                       dev_of((pos + n - dr) % n)).wait_recv()
                new = recv[h, s] + own[...]
                if s < n - 2:
                    acc[h, s] = new
                else:
                    put(h, new)

        steps.append((start, finish))
    return steps


def ring_ag_steps(n, pos, dev_of, mine, dst, sems, sends):
    half = mine.shape[0] // 2
    dirs = (1, n - 1)
    steps = []
    for s in range(n - 1):
        def start(s=s):
            if s == 0:
                dst[pos] = mine[...]
            for h, dr in enumerate(dirs):
                k = (pos + s * (n - dr)) % n
                rows = pl.ds(h * half, half)
                source = mine.at[rows] if s == 0 else dst.at[k, rows]
                cp = remote(source, dst.at[k, rows], sems.at[h, 0, s], sems.at[h, 1, s], dev_of((pos + dr) % n))
                cp.start()
                sends.append(cp)

        def finish(s=s):
            for h, dr in enumerate(dirs):
                k2 = (pos + (s + 1) * (n - dr)) % n
                rows = pl.ds(h * half, half)
                remote(mine.at[rows], dst.at[k2, rows], sems.at[h, 0, s], sems.at[h, 1, s],
                       dev_of((pos + n - dr) % n)).wait_recv()

        steps.append((start, finish))
    return steps


def direct_step(n, pos, dev_of, src_of, slot_of, send_sems, recv_sems, sends, after):
    def start():
        for d in range(1, n):
            c = (pos + d) % n
            cp = remote(src_of(c), slot_of(pos), send_sems.at[c], recv_sems.at[pos], dev_of(c))
            cp.start()
            sends.append(cp)
        slot_of(pos)[...] = src_of(pos)[...]

    def finish():
        for d in range(1, n):
            s = (pos + n - d) % n
            remote(src_of(s), slot_of(s), send_sems.at[s], recv_sems.at[s], dev_of(s)).wait_recv()
        after()

    return [(start, finish)]


def lat_sum_kernel(axis_names, ny, nlo, nhi, x_ref, out_ref, recv1, acc1, part1, recv2, part2, recv3, part3,
                   ag2, ag1, ring_sems, sems):
    lat = lax.axis_index("lat")
    my_y = lat % ny
    my_z = lat // ny
    my_lo = my_z % nlo
    my_hi = my_z // nlo
    rows = x_ref.shape[1]
    cols = part1.shape[-1]
    c2 = rows // nlo
    c3 = c2 // nhi

    def y_dev(c):
        return device_on(axis_names, {"lat": my_z * ny + c})

    def lo_dev(c):
        return device_on(axis_names, {"lat": (my_hi * nlo + c) * ny + my_y})

    def hi_dev(c):
        return device_on(axis_names, {"lat": (c * nlo + my_lo) * ny + my_y})

    def rows_of(c, size):
        return pl.ds(pl.multiple_of(c * size, size), size)

    barrier = pltpu.get_barrier_semaphore()
    for n, pos, dev_of in ((ny, my_y, y_dev), (nlo, my_lo, lo_dev), (nhi, my_hi, hi_dev)):
        for d in range(1, n):
            pl.semaphore_signal(barrier, 1, device_id=dev_of((pos + d) % n), device_id_type=MESH_ID)
    pl.semaphore_wait(barrier, (ny - 1) + (nlo - 1) + (nhi - 1))

    def summed(slots, n):
        total = slots[0]
        for s in range(1, n):
            total = total + slots[s]
        return total

    sends = []
    streams = []
    for q in range(2):
        width = pl.ds(q * cols, cols)
        half = rows // 2

        def put(h, value, q=q, half=half):
            part1[q, pl.ds(h * half, half)] = value

        def sum_lo(q=q):
            part2[q] = summed(recv2.at[q], nlo)

        def sum_hi(q=q):
            part3[q] = summed(recv3.at[q], nhi)

        steps = []
        steps += ring_rs_steps(ny, my_y, y_dev, x_ref.at[:, :, width], recv1.at[q], acc1.at[q],
                               ring_sems.at[q, 0], put, sends)
        steps += direct_step(nlo, my_lo, lo_dev, lambda c, q=q: part1.at[q, rows_of(c, c2)],
                             lambda c, q=q: recv2.at[q, c], sems.at[q, 0, 0], sems.at[q, 0, 1], sends, sum_lo)
        steps += direct_step(nhi, my_hi, hi_dev, lambda c, q=q: part2.at[q, rows_of(c, c3)],
                             lambda c, q=q: recv3.at[q, c], sems.at[q, 1, 0], sems.at[q, 1, 1], sends, sum_hi)
        steps += direct_step(nhi, my_hi, hi_dev, lambda c, q=q: part3.at[q],
                             lambda c, q=q: ag2.at[q, rows_of(c, c3)], sems.at[q, 2, 0], sems.at[q, 2, 1],
                             sends, lambda: None)
        steps += direct_step(nlo, my_lo, lo_dev, lambda c, q=q: ag2.at[q],
                             lambda c, q=q: ag1.at[q, rows_of(c, c2)], sems.at[q, 3, 0], sems.at[q, 3, 1],
                             sends, lambda: None)
        steps += ring_ag_steps(ny, my_y, y_dev, ag1.at[q], out_ref.at[:, :, width], ring_sems.at[q, 1], sends)
        streams.append(steps)

    lag = ny - 1
    total_slots = len(streams[0]) + lag
    for slot in range(total_slots):
        active = []
        for q, offset in ((0, 0), (1, lag)):
            i = slot - offset
            if 0 <= i < len(streams[q]):
                active.append(streams[q][i])
        for start, _ in active:
            start()
        for _, finish in active:
            finish()
    for cp in sends:
        cp.wait_send()


def lat_sum(x, axis_names, n_lat, cid):
    ny = 4 if n_lat % 4 == 0 else 1
    nz = n_lat // ny
    nlo = 4 if nz % 4 == 0 else nz
    nhi = nz // nlo
    chunks, rows, width = x.shape
    assert chunks == ny and rows % (8 * nz) == 0 and width % 256 == 0
    cols = width // 2
    c2 = rows // nlo
    c3 = c2 // nhi
    f32 = jnp.float32
    most = max(nlo, nhi)
    return pl.pallas_call(
        functools.partial(lat_sum_kernel, axis_names, ny, nlo, nhi),
        out_shape=jax.ShapeDtypeStruct(x.shape, x.dtype),
        in_specs=[pl.BlockSpec(memory_space=pltpu.VMEM)],
        out_specs=pl.BlockSpec(memory_space=pltpu.VMEM),
        scratch_shapes=[
            pltpu.VMEM((2, 2, ny - 1, rows // 2, cols), f32),
            pltpu.VMEM((2, 2, max(ny - 2, 1), rows // 2, cols), f32),
            pltpu.VMEM((2, rows, cols), f32),
            pltpu.VMEM((2, nlo, c2, cols), f32),
            pltpu.VMEM((2, c2, cols), f32),
            pltpu.VMEM((2, nhi, c3, cols), f32),
            pltpu.VMEM((2, c3, cols), f32),
            pltpu.VMEM((2, c2, cols), f32),
            pltpu.VMEM((2, rows, cols), f32),
            pltpu.SemaphoreType.DMA((2, 2, 2, 2, ny - 1)),
            pltpu.SemaphoreType.DMA((2, 4, 2, most)),
        ],
        compiler_params=pltpu.CompilerParams(
            collective_id=cid, has_side_effects=True, vmem_limit_bytes=48 * 1024 * 1024
        ),
    )(x)


def body(axis_names, n_lat, resid, dictionary, enc_bias, dec_bias, active_blocks, level_bounds):
    row_count, half_width = resid.shape
    lat_count = dictionary.shape[0]
    blocks_here = lat_count // 128
    lat_position = lax.axis_index("lat")
    first_block = lat_position * blocks_here
    local_ids = first_block + jnp.arange(blocks_here, dtype=jnp.int32)
    resid_full = resid.astype(jnp.float32)
    dict_blocks = dictionary.reshape(blocks_here, 128, half_width)

    partial_pre = lax.dot_general(
        resid, dictionary, (((1,), (1,)), ((), ())), preferred_element_type=jnp.float32
    )
    pre = axis_sum(partial_pre, axis_names, "wid", 2, 1) + enc_bias[None, :]
    hits = jnp.any(active_blocks[:, :, None] == local_ids[None, None, :], axis=1).astype(
        jnp.float32
    )
    act = (gelu_tanh(pre).reshape(row_count, blocks_here, 128) * hits[:, :, None]).astype(
        jnp.bfloat16
    )
    act_flat = act.reshape(row_count, lat_count)

    per_block = jnp.einsum(
        "tkc,kcd->ktd", act.reshape(row_count, blocks_here, 128), dict_blocks,
        preferred_element_type=jnp.float32,
    )
    keep = (local_ids[None, :] < level_bounds[:, None]).astype(jnp.float32)
    contrib = jnp.sum(keep[:, :, None, None] * per_block[None], axis=1)
    levels = lat_sum(contrib, axis_names, n_lat, 0)

    errors = dec_bias[None, None, :] + levels - resid_full[None]
    squares = jnp.sum(errors * errors, axis=(1, 2))
    running = errors[LEVELS - 1]
    cum_list = [running]
    for level in range(LEVELS - 2, -1, -1):
        running = running + errors[level]
        cum_list.append(running)
    cum_err = jnp.stack(cum_list[::-1]).astype(jnp.bfloat16)

    level_of = jnp.sum((level_bounds[None, :] <= local_ids[:, None]).astype(jnp.int32), axis=1)
    err_half = jnp.take(cum_err, level_of, axis=0)
    partial_adjoint = jnp.einsum(
        "ktd,kcd->tkc", err_half, dict_blocks, preferred_element_type=jnp.float32
    )
    loss_rows = jnp.zeros((8, lat_count), jnp.float32).at[0, :LEVELS].set(squares)
    adjoint_rows = jnp.concatenate([partial_adjoint.reshape(row_count, lat_count), loss_rows], axis=0)
    summed_rows = axis_sum(adjoint_rows, axis_names, "wid", 2, 2)
    g_act = summed_rows[:row_count]
    loss_tile = jnp.zeros((8, 128), jnp.float32).at[0, :LEVELS].set(summed_rows[row_count, :LEVELS])
    mask_full = jnp.broadcast_to(hits[:, :, None], (row_count, blocks_here, 128)).reshape(
        row_count, lat_count
    )
    _, pull = jax.vjp(gelu_tanh, pre)
    g_pre = pull(g_act * mask_full)[0].astype(jnp.bfloat16)
    left = jnp.concatenate(
        [err_half, jnp.broadcast_to(resid[None], (blocks_here, row_count, half_width))], axis=1
    )
    lt = jnp.transpose(left, (0, 2, 1))
    right = jnp.concatenate(
        [act.reshape(row_count, blocks_here, 128), g_pre.reshape(row_count, blocks_here, 128)], axis=0
    )
    rt = jnp.transpose(right, (1, 0, 2))
    tok_count = lax.axis_size("tok")
    grad_share, loss_sum = grad_ring(lt, rt, loss_tile, axis_names, "tok", tok_count, 4)
    total_sq = loss_sum[0, :LEVELS]
    level_losses = total_sq / (row_count * tok_count * half_width * lax.axis_size("wid"))
    return (level_losses, grad_share)


def solution(mesh):
    axis_names = tuple(mesh.axis_names)
    n_lat = mesh.shape["lat"]
    return jax.shard_map(
        functools.partial(body, axis_names, n_lat),
        mesh=mesh,
        in_specs=(P("tok", "wid"), P("lat", "wid"), P("lat"), P("wid"), P("tok", None), P()),
        out_specs=(P(), P(("wid", "tok"), "lat")),
        check_vma=False,
    )
```

```python
import functools

import jax
import jax.numpy as jnp
from jax import lax
from jax.experimental import pallas as pl
from jax.experimental.pallas import tpu as pltpu
from jax.sharding import PartitionSpec as P

LEVELS = 4
MESH_ID = pl.DeviceIdType.MESH


def gelu_tanh(value):
    return jax.nn.gelu(value, approximate=True)


def device_on(axis_names, moved):
    return tuple(moved[n] if n in moved else lax.axis_index(n) for n in axis_names)


def remote(src, dst, send_sem, recv_sem, device):
    return pltpu.make_async_remote_copy(
        src_ref=src, dst_ref=dst, send_sem=send_sem, recv_sem=recv_sem,
        device_id=device, device_id_type=MESH_ID,
    )


def gather_phase(n, pos, dev_of, src_of, slot_of, send_sems, recv_sems):
    sends = []
    for d in range(1, n):
        c = (pos + d) % n
        cp = remote(src_of(c), slot_of(pos), send_sems.at[c], recv_sems.at[pos], dev_of(c))
        cp.start()
        sends.append(cp)
    slot_of(pos)[...] = src_of(pos)[...]
    for d in range(1, n):
        s = (pos + n - d) % n
        remote(src_of(s), slot_of(s), send_sems.at[s], recv_sems.at[s], dev_of(s)).wait_recv()
    return sends


def ring_reduce_scatter(n, pos, dev_of, src, recv, acc, sems, put):
    half = src.shape[1] // 2
    dirs = (1, n - 1)
    sends = []
    for s in range(n - 1):
        for h, dr in enumerate(dirs):
            k = (pos + (s + 1) * (n - dr)) % n
            source = src.at[k, pl.ds(h * half, half)] if s == 0 else acc.at[h, s - 1]
            cp = remote(source, recv.at[h, s], sems.at[h, 0, s], sems.at[h, 1, s], dev_of((pos + dr) % n))
            cp.start()
            sends.append(cp)
        for h, dr in enumerate(dirs):
            k2 = (pos + (s + 2) * (n - dr)) % n
            own = src.at[k2, pl.ds(h * half, half)]
            remote(own, recv.at[h, s], sems.at[h, 0, s], sems.at[h, 1, s],
                   dev_of((pos + n - dr) % n)).wait_recv()
            new = recv[h, s] + own[...]
            if s < n - 2:
                acc[h, s] = new
            else:
                put(h, new)
    return sends


def ring_all_gather(n, pos, dev_of, mine, dst, sems):
    half = mine.shape[0] // 2
    dirs = (1, n - 1)
    dst[pos] = mine[...]
    sends = []
    for s in range(n - 1):
        for h, dr in enumerate(dirs):
            k = (pos + s * (n - dr)) % n
            rows = pl.ds(h * half, half)
            source = mine.at[rows] if s == 0 else dst.at[k, rows]
            cp = remote(source, dst.at[k, rows], sems.at[h, 0, s], sems.at[h, 1, s], dev_of((pos + dr) % n))
            cp.start()
            sends.append(cp)
        for h, dr in enumerate(dirs):
            k2 = (pos + (s + 1) * (n - dr)) % n
            rows = pl.ds(h * half, half)
            remote(mine.at[rows], dst.at[k2, rows], sems.at[h, 0, s], sems.at[h, 1, s],
                   dev_of((pos + n - dr) % n)).wait_recv()
    return sends


def grad_ring_kernel(axis_names, axis, n, lt_ref, rt_ref, loss_ref, out_ref, loss_out, part, recv, acc,
                     loss_slots, sems, loss_sems):
    me = lax.axis_index(axis)

    def dev_of(c):
        return device_on(axis_names, {axis: c})

    barrier = pltpu.get_barrier_semaphore()
    for d in range(1, n):
        pl.semaphore_signal(barrier, 1, device_id=dev_of((me + d) % n), device_id_type=MESH_ID)
    pl.semaphore_wait(barrier, n - 1)
    loss_sends = gather_phase(n, me, dev_of, lambda c: loss_ref, lambda c: loss_slots.at[c],
                              loss_sems.at[0], loss_sems.at[1])
    blocks, width, _ = lt_ref.shape
    rows = width // n
    lane = rt_ref.shape[2]

    def make_chunk(c):
        for k in range(blocks):
            part[c, :, pl.ds(k * lane, lane)] = jnp.dot(
                lt_ref[k, pl.ds(pl.multiple_of(c * rows, rows), rows), :], rt_ref[k],
                preferred_element_type=jnp.float32,
            )

    first = sorted({(n - 1) % n, 1 % n})
    later = [o for o in dict.fromkeys((2 % n, 0)) if o not in first]
    for o in first:
        make_chunk((me + o) % n)
    half = rows // 2

    def put(h, value):
        out_ref[pl.ds(h * half, half)] = value.astype(out_ref.dtype)

    sends = []
    steps = ring_rs_steps(n, me, dev_of, part, recv, acc, sems, put, sends)
    for i, (start, finish) in enumerate(steps):
        start()
        if i == 0:
            for o in later:
                make_chunk((me + o) % n)
        finish()
    total = loss_slots[0]
    for s in range(1, n):
        total = total + loss_slots[s]
    loss_out[...] = total
    for cp in sends + loss_sends:
        cp.wait_send()


def grad_ring(lt, rt, loss_tile, axis_names, axis, n, cid):
    blocks, width, _ = lt.shape
    lane = rt.shape[2]
    rows = width // n
    cols = blocks * lane
    f32 = jnp.float32
    return pl.pallas_call(
        functools.partial(grad_ring_kernel, axis_names, axis, n),
        out_shape=(jax.ShapeDtypeStruct((rows, cols), jnp.bfloat16),
                   jax.ShapeDtypeStruct(loss_tile.shape, f32)),
        in_specs=[pl.BlockSpec(memory_space=pltpu.VMEM)] * 3,
        out_specs=(pl.BlockSpec(memory_space=pltpu.VMEM), pl.BlockSpec(memory_space=pltpu.VMEM)),
        scratch_shapes=[
            pltpu.VMEM((n, rows, cols), f32),
            pltpu.VMEM((2, n - 1, rows // 2, cols), f32),
            pltpu.VMEM((2, max(n - 2, 1), rows // 2, cols), f32),
            pltpu.VMEM((n,) + loss_tile.shape, f32),
            pltpu.SemaphoreType.DMA((2, 2, n - 1)),
            pltpu.SemaphoreType.DMA((2, n)),
        ],
        compiler_params=pltpu.CompilerParams(
            collective_id=cid, has_side_effects=True, vmem_limit_bytes=56 * 1024 * 1024
        ),
    )(lt, rt, loss_tile)


def axis_sum_kernel(axis_names, axis, n, x_ref, out_ref, slots, send_sem, recv_sem):
    me = lax.axis_index(axis)

    def dev_of(c):
        return device_on(axis_names, {axis: c})

    barrier = pltpu.get_barrier_semaphore()
    for d in range(1, n):
        pl.semaphore_signal(barrier, 1, device_id=dev_of((me + d) % n), device_id_type=MESH_ID)
    pl.semaphore_wait(barrier, n - 1)
    sends = gather_phase(n, me, dev_of, lambda c: x_ref, lambda c: slots.at[c], send_sem, recv_sem)
    total = slots[0]
    for s in range(1, n):
        total = total + slots[s]
    out_ref[...] = total
    for cp in sends:
        cp.wait_send()


def axis_sum(x, axis_names, axis, n, cid):
    return pl.pallas_call(
        functools.partial(axis_sum_kernel, axis_names, axis, n),
        out_shape=jax.ShapeDtypeStruct(x.shape, x.dtype),
        in_specs=[pl.BlockSpec(memory_space=pltpu.VMEM)],
        out_specs=pl.BlockSpec(memory_space=pltpu.VMEM),
        scratch_shapes=[
            pltpu.VMEM((n,) + x.shape, x.dtype),
            pltpu.SemaphoreType.DMA((n,)),
            pltpu.SemaphoreType.DMA((n,)),
        ],
        compiler_params=pltpu.CompilerParams(collective_id=cid, has_side_effects=True),
    )(x)


def ring_rs_steps(n, pos, dev_of, src, recv, acc, sems, put, sends):
    half = src.shape[1] // 2
    dirs = (1, n - 1)
    steps = []
    for s in range(n - 1):
        def start(s=s):
            for h, dr in enumerate(dirs):
                k = (pos + (s + 1) * (n - dr)) % n
                source = src.at[k, pl.ds(h * half, half)] if s == 0 else acc.at[h, s - 1]
                cp = remote(source, recv.at[h, s], sems.at[h, 0, s], sems.at[h, 1, s], dev_of((pos + dr) % n))
                cp.start()
                sends.append(cp)

        def finish(s=s):
            for h, dr in enumerate(dirs):
                k2 = (pos + (s + 2) * (n - dr)) % n
                own = src.at[k2, pl.ds(h * half, half)]
                remote(own, recv.at[h, s], sems.at[h, 0, s], sems.at[h, 1, s],
                       dev_of((pos + n - dr) % n)).wait_recv()
                new = recv[h, s] + own[...]
                if s < n - 2:
                    acc[h, s] = new
                else:
                    put(h, new)

        steps.append((start, finish))
    return steps


def ring_ag_steps(n, pos, dev_of, mine, dst, sems, sends):
    half = mine.shape[0] // 2
    dirs = (1, n - 1)
    steps = []
    for s in range(n - 1):
        def start(s=s):
            if s == 0:
                dst[pos] = mine[...]
            for h, dr in enumerate(dirs):
                k = (pos + s * (n - dr)) % n
                rows = pl.ds(h * half, half)
                source = mine.at[rows] if s == 0 else dst.at[k, rows]
                cp = remote(source, dst.at[k, rows], sems.at[h, 0, s], sems.at[h, 1, s], dev_of((pos + dr) % n))
                cp.start()
                sends.append(cp)

        def finish(s=s):
            for h, dr in enumerate(dirs):
                k2 = (pos + (s + 1) * (n - dr)) % n
                rows = pl.ds(h * half, half)
                remote(mine.at[rows], dst.at[k2, rows], sems.at[h, 0, s], sems.at[h, 1, s],
                       dev_of((pos + n - dr) % n)).wait_recv()

        steps.append((start, finish))
    return steps


def direct_step(n, pos, dev_of, src_of, slot_of, send_sems, recv_sems, sends, after):
    def start():
        for d in range(1, n):
            c = (pos + d) % n
            cp = remote(src_of(c), slot_of(pos), send_sems.at[c], recv_sems.at[pos], dev_of(c))
            cp.start()
            sends.append(cp)
        slot_of(pos)[...] = src_of(pos)[...]

    def finish():
        for d in range(1, n):
            s = (pos + n - d) % n
            remote(src_of(s), slot_of(s), send_sems.at[s], recv_sems.at[s], dev_of(s)).wait_recv()
        after()

    return [(start, finish)]


def lat_sum_kernel(axis_names, ny, nlo, nhi, x_ref, out_ref, recv1, acc1, part1, recv2, part2, recv3, part3,
                   ag2, ag1, ring_sems, sems):
    lat = lax.axis_index("lat")
    my_y = lat % ny
    my_z = lat // ny
    my_lo = my_z % nlo
    my_hi = my_z // nlo
    rows = x_ref.shape[1]
    cols = part1.shape[-1]
    c2 = rows // nlo
    c3 = c2 // nhi

    def y_dev(c):
        return device_on(axis_names, {"lat": my_z * ny + c})

    def lo_dev(c):
        return device_on(axis_names, {"lat": (my_hi * nlo + c) * ny + my_y})

    def hi_dev(c):
        return device_on(axis_names, {"lat": (c * nlo + my_lo) * ny + my_y})

    def rows_of(c, size):
        return pl.ds(pl.multiple_of(c * size, size), size)

    barrier = pltpu.get_barrier_semaphore()
    for n, pos, dev_of in ((ny, my_y, y_dev), (nlo, my_lo, lo_dev), (nhi, my_hi, hi_dev)):
        for d in range(1, n):
            pl.semaphore_signal(barrier, 1, device_id=dev_of((pos + d) % n), device_id_type=MESH_ID)
    pl.semaphore_wait(barrier, (ny - 1) + (nlo - 1) + (nhi - 1))

    def summed(slots, n):
        total = slots[0]
        for s in range(1, n):
            total = total + slots[s]
        return total

    sends = []
    streams = []
    for q in range(2):
        width = pl.ds(q * cols, cols)
        half = rows // 2

        def put(h, value, q=q, half=half):
            part1[q, pl.ds(h * half, half)] = value

        def sum_lo(q=q):
            part2[q] = summed(recv2.at[q], nlo)

        def sum_hi(q=q):
            part3[q] = summed(recv3.at[q], nhi)

        steps = []
        steps += ring_rs_steps(ny, my_y, y_dev, x_ref.at[:, :, width], recv1.at[q], acc1.at[q],
                               ring_sems.at[q, 0], put, sends)
        steps += direct_step(nlo, my_lo, lo_dev, lambda c, q=q: part1.at[q, rows_of(c, c2)],
                             lambda c, q=q: recv2.at[q, c], sems.at[q, 0, 0], sems.at[q, 0, 1], sends, sum_lo)
        steps += direct_step(nhi, my_hi, hi_dev, lambda c, q=q: part2.at[q, rows_of(c, c3)],
                             lambda c, q=q: recv3.at[q, c], sems.at[q, 1, 0], sems.at[q, 1, 1], sends, sum_hi)
        steps += direct_step(nhi, my_hi, hi_dev, lambda c, q=q: part3.at[q],
                             lambda c, q=q: ag2.at[q, rows_of(c, c3)], sems.at[q, 2, 0], sems.at[q, 2, 1],
                             sends, lambda: None)
        steps += direct_step(nlo, my_lo, lo_dev, lambda c, q=q: ag2.at[q],
                             lambda c, q=q: ag1.at[q, rows_of(c, c2)], sems.at[q, 3, 0], sems.at[q, 3, 1],
                             sends, lambda: None)
        steps += ring_ag_steps(ny, my_y, y_dev, ag1.at[q], out_ref.at[:, :, width], ring_sems.at[q, 1], sends)
        streams.append(steps)

    lag = ny
    total_slots = len(streams[0]) + lag
    for slot in range(total_slots):
        active = []
        for q, offset in ((0, 0), (1, lag)):
            i = slot - offset
            if 0 <= i < len(streams[q]):
                active.append(streams[q][i])
        for start, _ in active:
            start()
        for _, finish in active:
            finish()
    for cp in sends:
        cp.wait_send()


def lat_sum(x, axis_names, n_lat, cid):
    ny = 4 if n_lat % 4 == 0 else 1
    nz = n_lat // ny
    nlo = 4 if nz % 4 == 0 else nz
    nhi = nz // nlo
    chunks, rows, width = x.shape
    assert chunks == ny and rows % (8 * nz) == 0 and width % 256 == 0
    cols = width // 2
    c2 = rows // nlo
    c3 = c2 // nhi
    f32 = jnp.float32
    most = max(nlo, nhi)
    return pl.pallas_call(
        functools.partial(lat_sum_kernel, axis_names, ny, nlo, nhi),
        out_shape=jax.ShapeDtypeStruct(x.shape, x.dtype),
        in_specs=[pl.BlockSpec(memory_space=pltpu.VMEM)],
        out_specs=pl.BlockSpec(memory_space=pltpu.VMEM),
        scratch_shapes=[
            pltpu.VMEM((2, 2, ny - 1, rows // 2, cols), f32),
            pltpu.VMEM((2, 2, max(ny - 2, 1), rows // 2, cols), f32),
            pltpu.VMEM((2, rows, cols), f32),
            pltpu.VMEM((2, nlo, c2, cols), f32),
            pltpu.VMEM((2, c2, cols), f32),
            pltpu.VMEM((2, nhi, c3, cols), f32),
            pltpu.VMEM((2, c3, cols), f32),
            pltpu.VMEM((2, c2, cols), f32),
            pltpu.VMEM((2, rows, cols), f32),
            pltpu.SemaphoreType.DMA((2, 2, 2, 2, ny - 1)),
            pltpu.SemaphoreType.DMA((2, 4, 2, most)),
        ],
        compiler_params=pltpu.CompilerParams(
            collective_id=cid, has_side_effects=True, vmem_limit_bytes=48 * 1024 * 1024
        ),
    )(x)


def body(axis_names, n_lat, resid, dictionary, enc_bias, dec_bias, active_blocks, level_bounds):
    row_count, half_width = resid.shape
    lat_count = dictionary.shape[0]
    blocks_here = lat_count // 128
    lat_position = lax.axis_index("lat")
    first_block = lat_position * blocks_here
    local_ids = first_block + jnp.arange(blocks_here, dtype=jnp.int32)
    resid_full = resid.astype(jnp.float32)
    dict_blocks = dictionary.reshape(blocks_here, 128, half_width)

    partial_pre = lax.dot_general(
        resid, dictionary, (((1,), (1,)), ((), ())), preferred_element_type=jnp.float32
    )
    pre = axis_sum(partial_pre, axis_names, "wid", 2, 1) + enc_bias[None, :]
    hits = jnp.any(active_blocks[:, :, None] == local_ids[None, None, :], axis=1).astype(
        jnp.float32
    )
    act = (gelu_tanh(pre).reshape(row_count, blocks_here, 128) * hits[:, :, None]).astype(
        jnp.bfloat16
    )
    act_flat = act.reshape(row_count, lat_count)

    per_block = jnp.einsum(
        "tkc,kcd->ktd", act.reshape(row_count, blocks_here, 128), dict_blocks,
        preferred_element_type=jnp.float32,
    )
    keep = (local_ids[None, :] < level_bounds[:, None]).astype(jnp.float32)
    contrib = jnp.sum(keep[:, :, None, None] * per_block[None], axis=1)
    levels = lat_sum(contrib, axis_names, n_lat, 0)

    errors = dec_bias[None, None, :] + levels - resid_full[None]
    squares = jnp.sum(errors * errors, axis=(1, 2))
    running = errors[LEVELS - 1]
    cum_list = [running]
    for level in range(LEVELS - 2, -1, -1):
        running = running + errors[level]
        cum_list.append(running)
    cum_err = jnp.stack(cum_list[::-1]).astype(jnp.bfloat16)

    level_of = jnp.sum((level_bounds[None, :] <= local_ids[:, None]).astype(jnp.int32), axis=1)
    err_half = jnp.take(cum_err, level_of, axis=0)
    partial_adjoint = jnp.einsum(
        "ktd,kcd->tkc", err_half, dict_blocks, preferred_element_type=jnp.float32
    )
    loss_rows = jnp.zeros((8, lat_count), jnp.float32).at[0, :LEVELS].set(squares)
    adjoint_rows = jnp.concatenate([partial_adjoint.reshape(row_count, lat_count), loss_rows], axis=0)
    summed_rows = axis_sum(adjoint_rows, axis_names, "wid", 2, 2)
    g_act = summed_rows[:row_count]
    loss_tile = jnp.zeros((8, 128), jnp.float32).at[0, :LEVELS].set(summed_rows[row_count, :LEVELS])
    mask_full = jnp.broadcast_to(hits[:, :, None], (row_count, blocks_here, 128)).reshape(
        row_count, lat_count
    )
    _, pull = jax.vjp(gelu_tanh, pre)
    g_pre = pull(g_act * mask_full)[0].astype(jnp.bfloat16)
    left = jnp.concatenate(
        [err_half, jnp.broadcast_to(resid[None], (blocks_here, row_count, half_width))], axis=1
    )
    lt = jnp.transpose(left, (0, 2, 1))
    right = jnp.concatenate(
        [act.reshape(row_count, blocks_here, 128), g_pre.reshape(row_count, blocks_here, 128)], axis=0
    )
    rt = jnp.transpose(right, (1, 0, 2))
    tok_count = lax.axis_size("tok")
    grad_share, loss_sum = grad_ring(lt, rt, loss_tile, axis_names, "tok", tok_count, 4)
    total_sq = loss_sum[0, :LEVELS]
    level_losses = total_sq / (row_count * tok_count * half_width * lax.axis_size("wid"))
    return (level_losses, grad_share)


def solution(mesh):
    axis_names = tuple(mesh.axis_names)
    n_lat = mesh.shape["lat"]
    return jax.shard_map(
        functools.partial(body, axis_names, n_lat),
        mesh=mesh,
        in_specs=(P("tok", "wid"), P("lat", "wid"), P("lat"), P("wid"), P("tok", None), P()),
        out_specs=(P(), P(("wid", "tok"), "lat")),
        check_vma=False,
    )
```
